32 devices in a mesh: energy: 2 (over x), slab: 8 (over z, y), row: 2 (over core).
Axes of the slice: x: 2, y: 2, z: 4, core: 2. Of those that a mesh axis runs over, the one named last changes fastest.
Arguments:
- green_blocks: bfloat16 [2, 12288, 768], P(None, ('energy', 'slab', 'row')), parts along dimension 1, may hold values from -3 to 3
- coupling: bfloat16 [2, 1024, 128], P(None, 'slab'), may hold values from -2 to 2
- source: bfloat16 [2, 12288, 128], P(None, ('energy', 'slab', 'row')), parts along dimension 1, may hold values from -6 to 6
- interior_count: int32 [8], P('slab'), may hold values from 256 to 512, as said below
Outputs:
- solution: float32 [2, 12288, 128], P(None, ('energy', 'slab', 'row')), parts along dimension 1
The draws below stay inside these ranges and needn't reach their ends.
There are 2 independent parts, one for each index of `energy`. The reference program is written for one: setup_inputs(seed, part) draws one part's arguments, and reference() takes and returns one part's arrays. A program takes and returns all parts, laid end to end along the dimension named above; an argument that names none is the same for every part. Nothing has to cross between parts.
Inputs may be any that keep to these rules, and one draw needn't show every extreme that they name: `interior_count`: some slab has exactly 512 live interior orbitals.
All inputs are finite; a program needn't handle non-finite values.
Results may differ from the reference program's by a relative error of at most 0.0095.
Values may be sent and summed in bfloat16 or wider, within the bound.
No kernel may reach another device: no remote copies, remote signals or barrier semaphores. Data moves between devices by JAX's collectives and lax.ppermute only.
A program may use at most 128 MiB of HBM per device.

```python
import math
import jax
import jax.numpy as jnp
from jax import lax

ORB = 768
IFC = 128
NRHS = 128
WIRE_SLABS = 8


def draw_green_blocks(key, part):
    random_keys = jax.random.split(jax.random.fold_in(key, 101), 9)
    noise = jax.random.truncated_normal(random_keys[0], -4.0, 4.0, (2, WIRE_SLABS, ORB, ORB)) * (0.3 / math.sqrt(ORB))
    position = jnp.arange(ORB)
    corner = (position[:, None] >= ORB - IFC) & (position[None, :] < IFC)
    noise = noise * jnp.where(corner, 0.3, 1.0)
    diag_real = jax.random.uniform(random_keys[1], (WIRE_SLABS, ORB), minval=0.6, maxval=1.4)
    diag_imag = jax.random.uniform(random_keys[2], (WIRE_SLABS, ORB), minval=-0.4, maxval=0.4)
    unit_orb = jnp.eye(ORB, dtype=jnp.float32)
    result = noise + jnp.stack([diag_real, diag_imag])[:, :, :, None] * unit_orb
    slow_share = 0.5
    slow = jax.random.uniform(random_keys[3], (IFC,)) < slow_share
    gradual_rate = jax.random.uniform(random_keys[4], (WIRE_SLABS, IFC), minval=0.93, maxval=0.97)
    sudden_spike = jax.random.uniform(random_keys[5], (WIRE_SLABS, 1)) < 0.06
    gradual_rate = gradual_rate * jnp.where(sudden_spike, 0.6, 1.0)
    fast_rate = jnp.exp(jax.random.uniform(random_keys[6], (WIRE_SLABS, IFC), minval=math.log(0.15), maxval=math.log(0.6)))
    rate = jnp.where(slow[None, :], gradual_rate, fast_rate)
    unit_ifc = jnp.eye(IFC, dtype=jnp.float32)
    phase_lf = jax.random.uniform(random_keys[7], (WIRE_SLABS, IFC), minval=-math.pi, maxval=math.pi)
    phase_fl = jax.random.uniform(random_keys[8], (WIRE_SLABS, IFC), minval=-math.pi, maxval=math.pi)
    link_lf = jnp.stack([rate * jnp.cos(phase_lf), rate * jnp.sin(phase_lf)])[:, :, :, None] * unit_ifc
    link_fl = jnp.stack([rate * jnp.cos(phase_fl), rate * jnp.sin(phase_fl)])[:, :, :, None] * unit_ifc
    result = result + jnp.pad(link_lf, ((0, 0), (0, 0), (ORB - IFC, 0), (0, ORB - IFC)))
    result = result + jnp.pad(link_fl, ((0, 0), (0, 0), (0, ORB - IFC), (ORB - IFC, 0)))
    return result.reshape(2, WIRE_SLABS * ORB, ORB).astype(jnp.bfloat16)


def draw_coupling(key, part):
    random_keys = jax.random.split(jax.random.fold_in(key, 202), 2)
    phase = jax.random.uniform(random_keys[0], (WIRE_SLABS, IFC), minval=-math.pi, maxval=math.pi)
    spread = 0.15
    noise = jax.random.truncated_normal(random_keys[1], -4.0, 4.0, (2, WIRE_SLABS, IFC, IFC)) * (spread / math.sqrt(IFC))
    unit_ifc = jnp.eye(IFC, dtype=jnp.float32)
    result = noise + jnp.stack([jnp.cos(phase), jnp.sin(phase)])[:, :, :, None] * unit_ifc
    return result.reshape(2, WIRE_SLABS * IFC, IFC).astype(jnp.bfloat16)


def draw_interior_count(key, part):
    random_keys = jax.random.split(jax.random.fold_in(key, 303), 2)
    minimum_level = (ORB - 2 * IFC) // 2
    highest = ORB - 2 * IFC
    counts = jax.random.randint(random_keys[0], (WIRE_SLABS,), minimum_level, highest + 1)
    chosen = jax.random.randint(random_keys[1], (), 0, WIRE_SLABS)
    return counts.at[chosen].set(highest).astype(jnp.int32)


def steps_of(stream_key, shape, pieces, smallest, high):
    def one(dim, shards_of):
        draws = jax.random.uniform(jax.random.fold_in(jax.random.fold_in(stream_key, 6), dim), (shards_of,), jnp.float32, smallest / len(pieces), high / len(pieces))
        return jnp.repeat(jnp.exp(draws), shape[dim] // shards_of).reshape((-1,) + (1,) * (len(shape) - dim - 1))

    level = one(*pieces[0])
    for cut in pieces[1:]:
        level = level * one(*cut)
    return level


def bell_draw(key, shape, scale, limit, cuts=(), kind=jnp.bfloat16):
    factor_of = steps_of(key, shape, cuts, -0.22, 0.18) if cuts else 1.0
    entries = jax.random.normal(key, shape, jnp.float32) * scale * factor_of
    return jnp.minimum(jnp.maximum(entries, -limit), limit).astype(kind)


def setup_inputs(seed: int = 0, part: int = 0) -> dict:
    key_list = jax.random.split(jax.random.key(seed), 5)
    part_keys = jax.random.split(jax.random.fold_in(key_list[4], part), 5)
    green_blocks = draw_green_blocks(jax.random.fold_in(jax.random.fold_in(key_list[4], part), 71), part)
    coupling = draw_coupling(jax.random.fold_in(key_list[4], 71), part)
    source = bell_draw(part_keys[2], (2, WIRE_SLABS * ORB, NRHS), 1.0, 6.0, ((1, 16),))
    interior_count = draw_interior_count(jax.random.fold_in(key_list[4], 71), part)
    return {"green_blocks": green_blocks, "coupling": coupling, "source": source, "interior_count": interior_count}


def multiply(matrix, operand):
    return jnp.matmul(matrix, operand, precision=lax.Precision.HIGHEST)


def complex_product(matrix, operand):
    real_part = multiply(matrix[0], operand[0]) - multiply(matrix[1], operand[1])
    imag_part = multiply(matrix[0], operand[1]) + multiply(matrix[1], operand[0])
    return jnp.stack([real_part, imag_part])


def adjoint(matrix):
    return jnp.stack([jnp.swapaxes(matrix[0], -1, -2), -jnp.swapaxes(matrix[1], -1, -2)])


def sweep_step(state, element):
    mapping, term = element
    return complex_product(mapping, state) + term, state


def reference(green_blocks, coupling, source, interior_count):
    green = green_blocks.astype(jnp.float32).reshape(2, WIRE_SLABS, ORB, ORB)
    slab_coupling = coupling.astype(jnp.float32).reshape(2, WIRE_SLABS, IFC, IFC)
    inject = source.astype(jnp.float32).reshape(2, WIRE_SLABS, ORB, NRHS)
    orbital = jnp.arange(ORB, dtype=jnp.int32)
    live = ((orbital[None, :] < IFC + interior_count[:, None]) | (orbital[None, :] >= ORB - IFC)).astype(jnp.float32)
    inject = inject * live[None, :, :, None]
    direct = complex_product(green, inject)
    edge_first = direct[:, :, :IFC]
    edge_last = direct[:, :, ORB - IFC:]
    zero_block = jnp.zeros((2, 1, IFC, IFC), jnp.float32)
    couple_next = jnp.concatenate([slab_coupling[:, :-1], zero_block], axis=1)
    couple_prev = jnp.concatenate([zero_block, slab_coupling[:, :-1]], axis=1)
    first_next = jnp.concatenate([edge_first[:, 1:], jnp.zeros((2, 1, IFC, NRHS), jnp.float32)], axis=1)
    green_ff = green[:, :, :IFC, :IFC]
    green_fl = green[:, :, :IFC, ORB - IFC:]
    green_lf = green[:, :, ORB - IFC:, :IFC]
    green_ll = green[:, :, ORB - IFC:, ORB - IFC:]
    forward_map = complex_product(green_lf, adjoint(couple_prev))
    forward_term = edge_last + complex_product(green_ll, complex_product(couple_next, first_next))
    start = jnp.zeros((2, IFC, NRHS), jnp.float32)
    _, preceding_slab = lax.scan(sweep_step, start, (jnp.moveaxis(forward_map, 1, 0), jnp.moveaxis(forward_term, 1, 0)))
    preceding_slab = jnp.moveaxis(preceding_slab, 0, 1)
    lower = complex_product(adjoint(couple_prev), preceding_slab)
    reverse_mapping = complex_product(green_fl, couple_next)
    backward_term = edge_first + complex_product(green_ff, lower)
    _, after = lax.scan(sweep_step, start, (jnp.moveaxis(reverse_mapping, 1, 0), jnp.moveaxis(backward_term, 1, 0)), reverse=True)
    after = jnp.moveaxis(after, 0, 1)
    upper = complex_product(couple_next, after)
    lower_round = lax.optimization_barrier(lower.astype(jnp.bfloat16)).astype(jnp.float32)
    upper_round = lax.optimization_barrier(upper.astype(jnp.bfloat16)).astype(jnp.float32)
    result = direct + complex_product(green[:, :, :, :IFC], lower_round) + complex_product(green[:, :, :, ORB - IFC:], upper_round)
    result = result * live[None, :, :, None]
    return result.reshape(2, WIRE_SLABS * ORB, NRHS)
```

```python
import jax
import jax.numpy as jnp
from jax import lax
from jax.experimental import pallas as pl
from jax.experimental.pallas import tpu as pltpu
from jax.sharding import PartitionSpec as P


F32 = jnp.float32
BF16 = jnp.bfloat16
GROUP = 4


def split(x):
    high = x.astype(BF16)
    return high, (x - high.astype(F32)).astype(BF16)


def dot(a, b):
    return jnp.dot(a, b, preferred_element_type=F32)


def turned(x):
    half = x.shape[1] // 2
    if half % 128 == 0:
        return jnp.concatenate([-x[:, half:], x[:, :half]], axis=1)
    lane = lax.broadcasted_iota(jnp.int32, x.shape, 1)
    rolled = pltpu.roll(x, half, 1)
    return jnp.where(lane < half, -rolled, rolled)


def stacked(x):
    return jnp.concatenate([x, turned(x)], axis=0)


def apply_exact(matrix, x):
    high, low = split(stacked(x))
    return dot(matrix, high) + dot(matrix, low)


def apply_rounded(matrix, x):
    return dot(matrix, stacked(x.astype(F32)).astype(BF16))


def ppermute_pairs(x, axis, pairs):
    return lax.ppermute(x, axis, pairs)


def edge_kernel(place, green, edge_other, source_own, source_other, direct, vectors):
    row, count, width = place[0], place[1], place[2]
    shard_rows = green.shape[1]
    surface = edge_other.shape[1]
    columns = source_own.shape[2]
    orbitals = 2 * shard_rows
    first_own = row == 0

    def masked(part):
        own = source_own[part].astype(F32)
        other = source_other[part].astype(F32)
        whole = jnp.concatenate(
            [jnp.where(first_own, own, other), jnp.where(first_own, other, own)], axis=0
        )
        orbital = lax.broadcasted_iota(jnp.int32, whole.shape, 0)
        live = (orbital < surface + count) | (orbital >= orbitals - surface)
        return jnp.where(live, whole, 0.0)

    real, imag = masked(0), masked(1)
    upper = jnp.concatenate([real, imag], axis=1).astype(BF16)
    below = jnp.concatenate([-imag, real], axis=1).astype(BF16)
    own = dot(green[0], upper) + dot(green[1], below)
    other = dot(edge_other[0], upper) + dot(edge_other[1], below)
    direct[...] = own
    own_edge = jnp.where(first_own, own[:surface], own[shard_rows - surface :])
    lane = lax.broadcasted_iota(jnp.int32, (surface, columns), 1)
    half = columns // 2

    def half_columns(x):
        re, im = x[:, :columns], x[:, columns:]
        first = jnp.where(lane < half, re, pltpu.roll(im, half, 1))
        second = jnp.where(lane < half, pltpu.roll(re, half, 1), im)
        return jnp.where(first_own, first, second)

    first_rows = half_columns(jnp.where(first_own, own_edge, other))
    last_rows = half_columns(jnp.where(first_own, other, own_edge))
    vectors[0] = first_rows.astype(BF16)
    vectors[1] = last_rows.astype(BF16)


LF, LL, FF, FL, BN, BH = range(6)


def response_kernel(place, *refs):
    packs, (maps, block, alpha, delta, gamma, states, backs) = refs[: 2 * GROUP], refs[2 * GROUP :]
    row, member = place[0], place[1]
    size = packs[0].shape[1]
    for k in range(GROUP):
        mine, other = packs[2 * k], packs[2 * k + 1]
        slot = member ^ k

        def chosen(index, want):
            return jnp.where(row == want, mine[index].astype(F32), other[index].astype(F32))

        def put(name, re, im):
            maps[slot, name] = jnp.concatenate([re, im], axis=1).astype(BF16)

        put(FF, chosen(0, 0), chosen(1, 0))
        put(FL, chosen(2, 0), chosen(3, 0))
        put(LF, chosen(0, 1), chosen(1, 1))
        put(LL, chosen(2, 1), chosen(3, 1))
        b_re, b_im = chosen(4, 0), chosen(4, 1)
        put(BN, b_re, b_im)
        put(BH, b_re.T, -b_im.T)
    eye = (
        lax.broadcasted_iota(jnp.int32, (size, size), 0)
        == lax.broadcasted_iota(jnp.int32, (size, size), 1)
    ).astype(F32)
    unit = jnp.concatenate([eye, jnp.zeros_like(eye)], axis=1)
    u = unit
    for i in range(GROUP):
        states[i] = u
        u = apply_exact(maps[i, BH], apply_exact(maps[i, LF], u))
    block[0] = u
    back = jnp.concatenate([jnp.zeros_like(unit), unit], axis=1)
    backs[GROUP] = back
    for i in reversed(range(GROUP)):
        d, c = back[:, : 2 * size], back[:, 2 * size :]
        if i < GROUP - 1:
            d = apply_exact(maps[i, FL], apply_exact(maps[i, BN], d))
        c = apply_exact(maps[i, FL], apply_exact(maps[i, BN], c))
        d = d + apply_exact(maps[i, FF], states[i])
        back = jnp.concatenate([d, c], axis=1)
        backs[i] = back
    block[1] = back[:, 2 * size :]
    block[2] = back[:, : 2 * size]
    alpha[...] = states[member]
    own = backs[member + 1]
    delta[...] = own[:, : 2 * size]
    gamma[...] = own[:, 2 * size :]


def sweep_kernel(place, maps, v0, v1, v2, v3, n0, n1, n2, n3, out, pi, sigma, vectors, states, backs):
    member = place[1]
    for k, v in enumerate((v0, v1, v2, v3)):
        vectors[member ^ k] = v[...].astype(F32)
    next_first = sum(n[...].astype(F32) for n in (n0, n1, n2, n3))
    first = [vectors[i, 0] for i in range(GROUP)] + [next_first]
    last = [vectors[i, 1] for i in range(GROUP)]
    terms = [
        last[i] + apply_exact(maps[i, LL], apply_rounded(maps[i, BN], first[i + 1]))
        for i in range(GROUP)
    ]
    u = jnp.zeros_like(next_first)
    for i in range(GROUP):
        states[i] = u
        t = terms[i]
        if i:
            t = t + apply_exact(maps[i, LF], u)
        u = apply_exact(maps[i, BH], t)
    out[0] = u.astype(BF16)
    s = jnp.zeros_like(next_first)
    backs[GROUP] = s
    for i in reversed(range(GROUP)):
        term = first[i]
        if i:
            term = term + apply_exact(maps[i, FF], states[i])
        if i < GROUP - 1:
            term = term + apply_exact(maps[i, FL], apply_exact(maps[i, BN], s))
        s = term
        backs[i] = s
    out[1] = s.astype(BF16)
    pi[...] = states[member]
    sigma[...] = backs[member + 1]


def apply_wide(matrix, x):
    high, low = split(matrix)
    x_high, x_low = split(stacked(x))
    return dot(high, x_high) + dot(low, x_high) + dot(high, x_low)


def close_kernel(coupling, own, seen, block_seen, pi, sigma, alpha, delta, gamma, out):
    before = seen[0].astype(F32)
    entry = seen[1].astype(F32) + apply_rounded(block_seen[...], own[0])
    lower = pi[...] + apply_wide(alpha[...], before)
    after = sigma[...] + apply_wide(delta[...], before) + apply_wide(gamma[...], entry)
    b = jnp.concatenate([coupling[0], coupling[1]], axis=1)
    out[0] = lower.astype(BF16)
    out[1] = apply_exact(b, after).astype(BF16)


def final_kernel(place, green, direct, own, other, result):
    row, count = place[0], place[1]
    shard_rows, width = green.shape[1:]
    surface, columns = own.shape[1:]
    half = columns // 2
    lane = lax.broadcasted_iota(jnp.int32, (surface, columns), 1)

    def whole(index):
        mine, theirs = own[index].astype(F32), other[index].astype(F32)
        h0 = jnp.where(row == 0, mine, theirs)
        h1 = jnp.where(row == 0, theirs, mine)
        re = jnp.where(lane < half, h0, pltpu.roll(h1, half, 1))
        im = jnp.where(lane < half, pltpu.roll(h0, half, 1), h1)
        return jnp.concatenate([re, im], axis=1)

    def product(start, x):
        a = green[0, :, start : start + surface]
        b = green[1, :, start : start + surface]
        return dot(jnp.concatenate([a, b], axis=1), stacked(x).astype(BF16))

    total = direct[...] + product(0, whole(0)) + product(width - surface, whole(1))
    orbital = row * shard_rows + lax.broadcasted_iota(jnp.int32, total.shape, 0)
    live = (orbital < surface + count) | (orbital >= width - surface)
    total = jnp.where(live, total, 0.0)
    result[0] = total[:, :columns]
    result[1] = total[:, columns:]


SMEM = pl.BlockSpec(memory_space=pltpu.SMEM)
VMEM = pl.BlockSpec(memory_space=pltpu.VMEM)


def call(kernel, name, outs, scratch=(), scalars=True):
    def run(*args):
        specs = [SMEM if scalars and i == 0 else VMEM for i in range(len(args))]
        return pl.pallas_call(
            kernel,
            name=name,
            in_specs=specs,
            out_specs=[VMEM] * len(outs),
            out_shape=[jax.ShapeDtypeStruct(s, d) for s, d in outs],
            scratch_shapes=[pltpu.VMEM(s, d) for s, d in scratch],
        )(*args)

    return run


def wide(a, b):
    n = a.shape[1] // 2
    m = b.shape[1] // 2

    def mul(x, y):
        return jnp.dot(x, y, preferred_element_type=F32, precision=lax.Precision.HIGHEST)

    ar, ai, br, bi = a[:, :n], a[:, n:], b[:, :m], b[:, m:]
    return jnp.concatenate([mul(ar, br) - mul(ai, bi), mul(ar, bi) + mul(ai, br)], axis=1)


def body(green_blocks, coupling, source, interior_count):
    shard_rows = green_blocks.shape[1]
    width = green_blocks.shape[2]
    surface = coupling.shape[1]
    columns = source.shape[2]
    row = lax.axis_index("row")
    slab = lax.axis_index("slab")
    slabs = lax.axis_size("slab")
    member = slab % GROUP
    swap = [(0, 1), (1, 0)]

    def across(x):
        return lax.ppermute(x, "row", swap)

    def partner(x, bit):
        return lax.ppermute(x, "slab", [(i, i ^ bit) for i in range(slabs)])

    scalars = jnp.stack([row, interior_count[0], jnp.int32(width)]).astype(jnp.int32)
    places = jnp.stack([row, member]).astype(jnp.int32)

    offset = row * (shard_rows - surface)
    edge = lax.dynamic_slice_in_dim(green_blocks, offset, surface, 1)
    b_part = lax.dynamic_slice_in_dim(coupling, row, 1, 0)
    b_part = jnp.where(slab < slabs - 1, b_part, jnp.zeros_like(b_part))
    pack = jnp.concatenate([edge[:, :, :surface], edge[:, :, width - surface :], b_part], axis=0)
    source_other = across(source)
    edge_other = across(edge)
    packs = [pack] + [partner(pack, k) for k in range(1, GROUP)]

    direct, vectors = call(
        edge_kernel,
        "edges",
        [((shard_rows, 2 * columns), F32), ((2, surface, columns), BF16)],
    )(scalars, green_blocks, edge_other, source, source_other)

    both = []
    for p in packs:
        both += [p, across(p)]
    square = (surface, 2 * surface)
    maps, block, alpha, delta, gamma = call(
        response_kernel,
        "responses",
        [((GROUP, 6) + square, BF16), ((3,) + square, F32), (square, F32), (square, F32), (square, F32)],
        [((GROUP,) + square, F32), ((GROUP + 1, surface, 4 * surface), F32)],
    )(places, *both)

    gathered = [vectors] + [partner(vectors, k) for k in range(1, GROUP)]
    upcoming = [
        lax.ppermute(
            vectors[0], "slab", [(g + GROUP, g + k) for g in range(0, slabs - GROUP, GROUP)]
        )
        for k in range(GROUP)
    ]
    half_shape = (surface, columns)
    own, pi, sigma = call(
        sweep_kernel,
        "sweeps",
        [((2,) + half_shape, BF16), (half_shape, F32), (half_shape, F32)],
        [((GROUP, 2) + half_shape, F32), ((GROUP,) + half_shape, F32), ((GROUP + 1,) + half_shape, F32)],
    )(places, maps, *gathered, *upcoming)

    bit = GROUP
    if 2 * bit < slabs:
        own = own.astype(F32)
    while 2 * bit < slabs:
        right = (slab // bit) % 2 == 1
        seen_block, seen = partner(block, bit), partner(own, bit)
        x_block = jnp.where(right, seen_block, block)
        y_block = jnp.where(right, block, seen_block)
        x_own = jnp.where(right, seen, own)
        y_own = jnp.where(right, own, seen)
        entry = wide(y_block[2], x_own[0]) + y_own[1]
        through = wide(y_block[2], x_block[0])
        pi = pi + jnp.where(right, wide(alpha, x_own[0]), 0.0)
        sigma = sigma + jnp.where(right, wide(delta, x_own[0]), wide(gamma, entry))
        delta = jnp.where(right, wide(delta, x_block[0]), delta + wide(gamma, through))
        alpha = jnp.where(right, wide(alpha, x_block[0]), alpha)
        gamma = jnp.where(right, gamma, wide(gamma, y_block[1]))
        own = jnp.stack(
            [wide(y_block[0], x_own[0]) + y_own[0], x_own[1] + wide(x_block[1], entry)]
        )
        block = jnp.stack(
            [
                wide(y_block[0], x_block[0]),
                wide(x_block[1], y_block[1]),
                x_block[2] + wide(x_block[1], through),
            ]
        )
        bit *= 2
    own = own.astype(BF16)
    half = slabs // 2
    up = [(i, i + half) for i in range(half)]
    down = [(i + half, i) for i in range(half)]
    block_seen = lax.ppermute(block[2].astype(BF16), "slab", down)
    seen = jnp.stack([lax.ppermute(own[0], "slab", up), lax.ppermute(own[1], "slab", down)])
    (ends,) = call(
        close_kernel, "close", [((2, surface, columns), BF16)], scalars=False
    )(coupling, own, seen, block_seen, pi, sigma, alpha, delta, gamma)
    (result,) = call(
        final_kernel, "final", [((2, shard_rows, columns), F32)]
    )(scalars, green_blocks, direct, ends, across(ends))
    return result


def solution(mesh):
    placed = (
        P(None, ("energy", "slab", "row"), None),
        P(None, "slab", None),
        P(None, ("energy", "slab", "row"), None),
        P("slab"),
    )
    return jax.shard_map(
        body,
        mesh=mesh,
        in_specs=placed,
        out_specs=P(None, ("energy", "slab", "row"), None),
        check_vma=False,
    )
```

```python
import jax
import jax.numpy as jnp
from jax import lax
from jax.experimental import pallas as pl
from jax.experimental.pallas import tpu as pltpu
from jax.sharding import PartitionSpec as P


F32 = jnp.float32
BF16 = jnp.bfloat16
GROUP = 4
FF, FL, LF, LL, BN = range(5)


def contract(x, matrix, across):
    return lax.dot_general(
        x, matrix, (((1,), (1 if across else 0,)), ((), ())), preferred_element_type=F32
    )


def split(x):
    high = x.astype(BF16)
    return high, (x - high.astype(F32)).astype(BF16)


def apply(real_form, x, across=True):
    high, low = split(x)
    both = contract(jnp.concatenate([high, low], axis=0), real_form, across)
    return both[: x.shape[0]] + both[x.shape[0] :]


def apply_short(real_form, x, across=True):
    return contract(x.astype(BF16), real_form, across)


def turned(x):
    half = x.shape[1] // 2
    return jnp.concatenate([-x[:, half:], x[:, :half]], axis=1)


def stacked(x):
    return jnp.concatenate([x, turned(x)], axis=0)


def apply_computed(columns, x):
    high, low = split(stacked(columns))
    x_high, x_low = split(x)
    both = contract(jnp.concatenate([x_high, x_low], axis=0), high, False)
    return both[: x.shape[0]] + both[x.shape[0] :] + contract(x_high, low, False)


def pack_kernel(green, coupling, edge, pack, sems):
    row = lax.axis_index("row")
    shard_rows, width = green.shape[1:]
    surface = edge.shape[1]
    rows = pl.ds(pl.multiple_of(row * (shard_rows - surface), surface), surface)
    copies = [
        pltpu.make_async_copy(green.at[:, rows, pl.ds(0, surface)], pack.at[pl.ds(0, 2)], sems.at[0]),
        pltpu.make_async_copy(
            green.at[:, rows, pl.ds(width - surface, surface)], pack.at[pl.ds(2, 2)], sems.at[1]
        ),
        pltpu.make_async_copy(coupling.at[pl.ds(row, 1)], pack.at[pl.ds(4, 1)], sems.at[2]),
        pltpu.make_async_copy(green.at[:, rows], edge, sems.at[3]),
    ]
    for c in copies:
        c.start()
    for c in copies:
        c.wait()


def edge_kernel(count, green, edge_other, source_own, source_other, direct, vectors):
    row = lax.axis_index("row")
    shard_rows = green.shape[1]
    surface = edge_other.shape[1]
    columns = source_own.shape[2]
    orbitals = 2 * shard_rows
    first_own = row == 0

    def masked(part):
        own = source_own[part].astype(F32)
        other = source_other[part].astype(F32)
        whole = jnp.concatenate(
            [jnp.where(first_own, own, other), jnp.where(first_own, other, own)], axis=0
        )
        orbital = lax.broadcasted_iota(jnp.int32, whole.shape, 0)
        live = (orbital < surface + count[0]) | (orbital >= orbitals - surface)
        return jnp.where(live, whole, 0.0)

    real, imag = masked(0), masked(1)
    above = jnp.concatenate([real, imag], axis=1).astype(BF16)
    below = jnp.concatenate([-imag, real], axis=1).astype(BF16)
    other = contract(edge_other[0], above, False) + contract(edge_other[1], below, False)
    own = contract(green[0], above, False) + contract(green[1], below, False)
    direct[...] = own
    own_edge = jnp.where(first_own, own[:surface], own[shard_rows - surface :])
    half = columns // 2

    def transposed(x):
        re, im = x[:, :columns].T, x[:, columns:].T
        whole = jnp.concatenate([re, im], axis=1)
        return jnp.where(first_own, whole[:half], whole[half:]).astype(BF16)

    own_t, other_t = transposed(own_edge), transposed(other)

    @pl.when(first_own)
    def _():
        vectors[:half] = own_t
        vectors[half:] = other_t

    @pl.when(row == 1)
    def _():
        vectors[:half] = other_t
        vectors[half:] = own_t


def maps_kernel(*refs):
    edge, edge_other, coupling = refs[:3]
    packs = refs[3 : 3 + 2 * (GROUP - 1)]
    maps, send, alpha, delta, last_term, block, states, backs = refs[3 + len(packs) :]
    row = lax.axis_index("row")
    slab = lax.axis_index("slab")
    slabs = lax.axis_size("slab")
    member = slab % GROUP
    size = coupling.shape[1]
    width = edge.shape[2]

    def put(slot, name, re, im):
        maps[slot, name, :size, :size] = re
        maps[slot, name, :size, size:] = -im
        maps[slot, name, size:, :size] = im
        maps[slot, name, size:, size:] = re

    def put_coupling(slot, re, im):
        known = slab - member + slot < slabs - 1
        put(slot, BN, jnp.where(known, re, jnp.zeros_like(re)), jnp.where(known, im, jnp.zeros_like(im)))

    def fill(first_is_own):
        f, l = (edge, edge_other) if first_is_own else (edge_other, edge)
        for name, ref, start in ((FF, f, 0), (FL, f, width - size), (LF, l, 0), (LL, l, width - size)):
            put(member, name, ref[0, :, start : start + size], ref[1, :, start : start + size])
        put_coupling(member, coupling[0], coupling[1])
        for k in range(1, GROUP):
            mine, other = packs[2 * k - 2], packs[2 * k - 1]
            f, l = (mine, other) if first_is_own else (other, mine)
            slot = member ^ k
            put(slot, FF, f[0], f[1])
            put(slot, FL, f[2], f[3])
            put(slot, LF, l[0], l[1])
            put(slot, LL, l[2], l[3])
            put_coupling(slot, f[4], l[4])

    @pl.when(row == 0)
    def _():
        fill(True)

    @pl.when(row == 1)
    def _():
        fill(False)

    eye = (
        lax.broadcasted_iota(jnp.int32, (size, size), 0)
        == lax.broadcasted_iota(jnp.int32, (size, size), 1)
    ).astype(F32)
    unit = jnp.concatenate([eye, jnp.zeros_like(eye)], axis=1)
    u = unit
    for i in range(GROUP):
        states[i] = u
        if i < GROUP - 1 or 2 * GROUP < slabs:
            t = apply(maps[i, LF], u) if i else apply_short(maps[i, LF], u)
            u = apply(maps[i, BN], t, False)
    block[0] = u
    s = apply(maps[GROUP - 1, FF], states[GROUP - 1])
    backs[GROUP] = jnp.zeros_like(unit)
    backs[GROUP - 1] = s
    for i in reversed(range(GROUP - 1)):
        s = apply(maps[i, FF], states[i]) + apply(maps[i, FL], apply(maps[i, BN], s))
        backs[i] = s
    block[1] = s
    w = apply_short(maps[GROUP - 1, BN], unit)
    w = apply(maps[GROUP - 1, BN], apply_short(maps[GROUP - 1, LL], w), False)
    last_term[...] = w
    send[...] = jnp.where(slab < slabs // 2, w, s).astype(BF16)
    alpha[...] = states[member]
    delta[...] = backs[member + 1]


def gamma_kernel(maps, gamma, whole, backs):
    member = lax.axis_index("slab") % GROUP
    size = gamma.shape[0]
    eye = (
        lax.broadcasted_iota(jnp.int32, (size, size), 0)
        == lax.broadcasted_iota(jnp.int32, (size, size), 1)
    ).astype(F32)
    unit = jnp.concatenate([eye, jnp.zeros_like(eye)], axis=1)
    backs[GROUP] = unit
    s = apply(maps[GROUP - 1, FL], apply_short(maps[GROUP - 1, BN], unit))
    backs[GROUP - 1] = s
    for i in reversed(range(GROUP - 1)):
        s = apply(maps[i, FL], apply(maps[i, BN], s))
        backs[i] = s
    whole[...] = s
    gamma[...] = backs[member + 1]


def sweep_kernel(maps, v0, v1, v2, v3, send, ends, pi, sigma, vectors, states, backs):
    slab = lax.axis_index("slab")
    member = slab % GROUP
    half = pi.shape[0]
    for k, v in enumerate((v0, v1, v2, v3)):
        vectors[member ^ k] = v[...]
    first = [vectors[i, :half] for i in range(GROUP)]
    last = [vectors[i, half:].astype(F32) for i in range(GROUP)]
    u = jnp.zeros(pi.shape, F32)
    states[0] = u
    for i in range(GROUP):
        t = last[i]
        if i < GROUP - 1:
            t = t + apply(maps[i, LL], apply_short(maps[i, BN], first[i + 1]))
        if i:
            states[i] = u
            t = t + apply(maps[i, LF], u)
        u = apply(maps[i, BN], t, False)
    s = jnp.zeros(pi.shape, F32)
    backs[GROUP] = s
    for i in reversed(range(GROUP)):
        term = first[i].astype(F32)
        if i:
            term = term + apply(maps[i, FF], states[i])
        if i < GROUP - 1:
            term = term + apply(maps[i, FL], apply(maps[i, BN], s))
        s = term
        backs[i] = s
    ends[0] = u
    ends[1] = s
    send[:half] = jnp.where(slab < lax.axis_size("slab") // 2, u, s).astype(BF16)
    send[half:] = first[0]
    pi[...] = states[member]
    sigma[...] = backs[member + 1]


def close_kernel(coupling, own_exit, first, seen, map_seen, last_term, pi, sigma, alpha, delta, gamma, out):
    size = coupling.shape[1]
    half = pi.shape[0]
    left = lax.axis_index("slab") < lax.axis_size("slab") // 2
    there = seen[:half].astype(F32)
    map_form = stacked(map_seen[...].astype(F32)).astype(BF16)
    b_re, b_im = coupling[0], coupling[1]
    b = jnp.concatenate(
        [jnp.concatenate([b_re, -b_im], axis=1), jnp.concatenate([b_im, b_re], axis=1)], axis=0
    )

    @pl.when(left)
    def _():
        leaving = own_exit[...] + apply_computed(last_term[...], seen[half:].astype(F32))
        entry = there + apply(map_form, leaving, False)
        after = sigma[...] + apply_computed(gamma[...], entry)
        out[:half] = pi[...].astype(BF16)
        out[half:] = apply(b, after).astype(BF16)

    @pl.when(jnp.logical_not(left))
    def _():
        before = there + apply_short(map_form, first[...], False)
        after = sigma[...] + apply_computed(delta[...], before)
        out[:half] = (pi[...] + apply_computed(alpha[...], before)).astype(BF16)
        out[half:] = apply(b, after).astype(BF16)


def final_kernel(count, green, direct, own, other, result, whole):
    row = lax.axis_index("row")
    shard_rows, width = green.shape[1:]
    half = own.shape[0] // 2
    columns = 2 * half
    surface = own.shape[1] // 2

    def place(first, second):
        for i in range(2):
            whole[i, :half] = first[i * half : (i + 1) * half]
            whole[i, half:] = second[i * half : (i + 1) * half]

    @pl.when(row == 0)
    def _():
        place(own, other)

    @pl.when(row == 1)
    def _():
        place(other, own)

    def product(start, x):
        g = jnp.concatenate(
            [green[0, :, start : start + surface], green[1, :, start : start + surface]], axis=1
        )
        x_re, x_im = x[:, :surface], x[:, surface:]
        form = jnp.concatenate(
            [jnp.concatenate([x_re, -x_im], axis=1), jnp.concatenate([x_im, x_re], axis=1)], axis=0
        )
        return contract(g, form, True)

    total = direct[...] + product(0, whole[0]) + product(width - surface, whole[1])
    orbital = row * shard_rows + lax.broadcasted_iota(jnp.int32, total.shape, 0)
    live = (orbital < surface + count[0]) | (orbital >= width - surface)
    total = jnp.where(live, total, 0.0)
    result[0] = total[:, :columns]
    result[1] = total[:, columns:]


S, V, H = (pl.BlockSpec(memory_space=m) for m in (pltpu.SMEM, pltpu.VMEM, pl.ANY))


def call(kernel, name, specs, outs, scratch, *args, keep=False):
    args = [
        pltpu.with_memory_space_constraint(a, pltpu.VMEM) if s is V else a
        for a, s in zip(args, specs, strict=True)
    ]
    kind = jax.ShapeDtypeStruct if keep else pltpu.VMEM
    return pl.pallas_call(
        kernel,
        name=name,
        in_specs=specs,
        out_specs=[V] * len(outs),
        out_shape=[kind(s, d) for s, d in outs],
        scratch_shapes=[pltpu.VMEM(*x) if isinstance(x, tuple) else x for x in scratch],
        compiler_params=pltpu.CompilerParams(vmem_limit_bytes=24 << 20),
    )(*args)


def compute(columns, x):
    size = columns.shape[1] // 2

    def mul(a, b):
        return jnp.dot(a, b, preferred_element_type=F32, precision=lax.Precision.HIGHEST)

    c_re, c_im = columns[:, :size], columns[:, size:]
    x_re, x_im = x[:, :size], x[:, size:]
    return jnp.concatenate([mul(x_re, c_re) - mul(x_im, c_im), mul(x_re, c_im) + mul(x_im, c_re)], axis=1)


def body(green_blocks, coupling, source, interior_count):
    shard_rows = green_blocks.shape[1]
    width = green_blocks.shape[2]
    surface = coupling.shape[1]
    columns = source.shape[2]
    half = columns // 2
    slab = lax.axis_index("slab")
    slabs = lax.axis_size("slab")

    def across(x):
        return lax.ppermute(x, "row", [(0, 1), (1, 0)])

    def partner(x, bit):
        return lax.ppermute(x, "slab", [(i, i ^ bit) for i in range(slabs)])

    square = (surface, 2 * surface)
    thin = (half, 2 * surface)
    edge, pack = call(
        pack_kernel,
        "pack",
        [H, H],
        [((2, surface, width), BF16), ((5, surface, surface), BF16)],
        [pltpu.SemaphoreType.DMA((4,))],
        green_blocks,
        coupling,
    )
    source_other = across(source)
    edge_other = across(edge)
    packs = [partner(pack, k) for k in range(1, GROUP)]
    direct, vectors = call(
        edge_kernel,
        "edges",
        [S, V, V, V, V],
        [((shard_rows, 2 * columns), F32), ((columns, 2 * surface), BF16)],
        [],
        interior_count,
        green_blocks,
        edge_other,
        source,
        source_other,
    )
    gathered = [partner(vectors, k) for k in range(1, GROUP)]
    both = []
    for p in packs:
        p, _ = lax.optimization_barrier((p, vectors))
        both += [p, across(p)]
    maps, send_map, alpha, delta, last_term, block = call(
        maps_kernel,
        "maps",
        [V] * (3 + len(both)),
        [((GROUP, 5, 2 * surface, 2 * surface), BF16), (square, BF16)]
        + [(square, F32)] * 3
        + [((2,) + square, F32)],
        [((GROUP,) + square, F32), ((GROUP + 1,) + square, F32)],
        edge,
        edge_other,
        coupling,
        *both,
    )
    send, ends, pi, sigma = call(
        sweep_kernel,
        "sweeps",
        [V] * (1 + GROUP),
        [((columns, 2 * surface), BF16), ((2,) + thin, F32), (thin, F32), (thin, F32)],
        [((GROUP, columns, 2 * surface), BF16), ((GROUP,) + thin, F32), ((GROUP + 1,) + thin, F32)],
        maps,
        vectors,
        *gathered,
    )
    gamma, back_whole = call(
        gamma_kernel,
        "gamma",
        [V],
        [(square, F32), (square, F32)],
        [((GROUP + 1,) + square, F32)],
        maps,
    )
    leave, first = ends[0], send[half:]
    bit = GROUP
    if 2 * bit < slabs:
        first = first.astype(F32)
        back = ends[1]
        a_map, d_map, c_map = block[0], block[1], back_whole
    while 2 * bit < slabs:
        right = (slab // bit) % 2 == 1

        def sides(own):
            seen = partner(own, bit)
            return jnp.where(right, seen, own), jnp.where(right, own, seen)

        (ax, ay), (cx, cy), (dx, dy) = sides(a_map), sides(c_map), sides(d_map)
        (wx, wy), (fx, fy) = sides(last_term), sides(first)
        (px, py), (qx, qy) = sides(leave), sides(back)
        middle = px + compute(wx, fy)
        entry = qy + compute(dy, middle)
        through = compute(dy, ax)
        pi = pi + jnp.where(right, compute(alpha, middle), 0.0)
        sigma = sigma + jnp.where(right, compute(delta, middle), compute(gamma, entry))
        delta = jnp.where(right, compute(delta, ax), delta + compute(gamma, through))
        alpha = jnp.where(right, compute(alpha, ax), alpha)
        gamma = jnp.where(right, gamma, compute(gamma, cy))
        leave, back = py + compute(ay, middle), qx + compute(cx, entry)
        a_map, c_map, d_map = compute(ay, ax), compute(cx, cy), dx + compute(cx, through)
        last_term, first = wy, fx
        bit *= 2
        if 2 * bit == slabs:
            left = slab < slabs // 2
            send = jnp.concatenate([jnp.where(left, leave, back), first], axis=0).astype(BF16)
            send_map = jnp.where(left, last_term, d_map).astype(BF16)
            first = first.astype(BF16)
    map_seen = partner(send_map, slabs // 2)
    seen = partner(send, slabs // 2)
    (closed,) = call(
        close_kernel,
        "close",
        [V] * 11,
        [((columns, 2 * surface), BF16)],
        [],
        coupling,
        leave,
        first,
        seen,
        map_seen,
        last_term,
        pi,
        sigma,
        alpha,
        delta,
        gamma,
    )
    (result,) = call(
        final_kernel,
        "final",
        [S, V, V, V, V],
        [((2, shard_rows, columns), F32)],
        [((2, columns, 2 * surface), BF16)],
        interior_count,
        green_blocks,
        direct,
        closed,
        across(closed),
        keep=True,
    )
    return result


def solution(mesh):
    placed = (
        P(None, ("energy", "slab", "row"), None),
        P(None, "slab", None),
        P(None, ("energy", "slab", "row"), None),
        P("slab"),
    )
    return jax.shard_map(
        body,
        mesh=mesh,
        in_specs=placed,
        out_specs=P(None, ("energy", "slab", "row"), None),
        check_vma=False,
    )
```

```python
import jax
import jax.numpy as jnp
from jax import lax
from jax.experimental import pallas as pl
from jax.experimental.pallas import tpu as pltpu
from jax.sharding import PartitionSpec as P


F32 = jnp.float32
BF16 = jnp.bfloat16
GROUP = 4
FF, FL, LF, LL, BN = range(5)


def contract(x, matrix, across):
    return lax.dot_general(
        x, matrix, (((1,), (1 if across else 0,)), ((), ())), preferred_element_type=F32
    )


def split(x):
    high = x.astype(BF16)
    return high, (x - high.astype(F32)).astype(BF16)


def apply(real_form, x, across=True):
    high, low = split(x)
    both = contract(jnp.concatenate([high, low], axis=0), real_form, across)
    return both[: x.shape[0]] + both[x.shape[0] :]


def apply_short(real_form, x, across=True):
    return contract(x.astype(BF16), real_form, across)


def turned(x):
    half = x.shape[1] // 2
    return jnp.concatenate([-x[:, half:], x[:, :half]], axis=1)


def stacked(x):
    return jnp.concatenate([x, turned(x)], axis=0)


def apply_computed(columns, x):
    high, low = split(stacked(columns))
    x_high, x_low = split(x)
    both = contract(jnp.concatenate([x_high, x_low], axis=0), high, False)
    return both[: x.shape[0]] + both[x.shape[0] :] + contract(x_high, low, False)


def pack_kernel(green, coupling, source, edge, pack, source_near, sems):
    row = lax.axis_index("row")
    shard_rows, width = green.shape[1:]
    surface = edge.shape[1]
    rows = pl.ds(pl.multiple_of(row * (shard_rows - surface), surface), surface)
    last = pl.ds(width - surface, surface)
    copies = [
        pltpu.make_async_copy(green.at[:, rows, pl.ds(0, surface)], pack.at[pl.ds(0, 2)], sems.at[0]),
        pltpu.make_async_copy(green.at[:, rows, last], pack.at[pl.ds(2, 2)], sems.at[1]),
        pltpu.make_async_copy(coupling.at[pl.ds(row, 1)], pack.at[pl.ds(4, 1)], sems.at[2]),
        pltpu.make_async_copy(green.at[:, rows], edge, sems.at[3]),
        pltpu.make_async_copy(source, source_near, sems.at[4]),
    ]
    for c in copies:
        c.start()
    for c in copies:
        c.wait()


def masked_source(count, own, other, surface):
    row = lax.axis_index("row")
    orbitals = 2 * own.shape[1]

    def masked(part):
        mine, theirs = own[part].astype(F32), other[part].astype(F32)
        whole = jnp.concatenate(
            [jnp.where(row == 0, mine, theirs), jnp.where(row == 0, theirs, mine)], axis=0
        )
        orbital = lax.broadcasted_iota(jnp.int32, whole.shape, 0)
        live = (orbital < surface + count[:1]) | (orbital >= orbitals - surface)
        return jnp.where(live, whole, 0.0)

    real, imag = masked(0), masked(1)
    return (
        jnp.concatenate([real, imag], axis=1).astype(BF16),
        jnp.concatenate([-imag, real], axis=1).astype(BF16),
    )


def edge_kernel(count, edge, edge_other, source_own, source_other, vectors):
    row = lax.axis_index("row")
    surface = edge.shape[1]
    columns = source_own.shape[2]
    half = columns // 2
    above, below = masked_source(count, source_own, source_other, surface)

    def surface_rows(blocks):
        x = contract(blocks[0], above, False) + contract(blocks[1], below, False)
        whole = jnp.concatenate([x[:, :columns].T, x[:, columns:].T], axis=1)
        return jnp.where(row == 0, whole[:half], whole[half:]).astype(BF16)

    own, other = surface_rows(edge), surface_rows(edge_other)

    @pl.when(row == 0)
    def _():
        vectors[:half] = own
        vectors[half:] = other

    @pl.when(row == 1)
    def _():
        vectors[:half] = other
        vectors[half:] = own


def direct_kernel(count, green, source_own, source_other, surfaces, direct):
    above, below = masked_source(count, source_own, source_other, surfaces.shape[1] // 2)
    direct[...] = contract(green[0], above, False) + contract(green[1], below, False)


def unit_columns(size):
    eye = (
        lax.broadcasted_iota(jnp.int32, (size, size), 0)
        == lax.broadcasted_iota(jnp.int32, (size, size), 1)
    ).astype(F32)
    return jnp.concatenate([eye, jnp.zeros_like(eye)], axis=1)


def solve_kernel(*refs):
    edge, edge_other, coupling = refs[:3]
    packs = refs[3 : 3 + 2 * (GROUP - 1)]
    given = refs[3 + len(packs) : 3 + len(packs) + GROUP]
    maps, send, here, after, last_term, leaving, entering, vectors, states, backs = refs[
        3 + len(packs) + GROUP :
    ]
    row = lax.axis_index("row")
    slab = lax.axis_index("slab")
    slabs = lax.axis_size("slab")
    member = slab % GROUP
    size = coupling.shape[1]
    width = edge.shape[2]
    half = vectors.shape[1] // 2

    def put(slot, name, re, im):
        maps[slot, name, :size, :size] = re
        maps[slot, name, :size, size:] = -im
        maps[slot, name, size:, :size] = im
        maps[slot, name, size:, size:] = re

    def put_coupling(slot, re, im):
        known = slab - member + slot < slabs - 1
        put(slot, BN, jnp.where(known, re, jnp.zeros_like(re)), jnp.where(known, im, jnp.zeros_like(im)))

    def fill(first_is_own):
        f, l = (edge, edge_other) if first_is_own else (edge_other, edge)
        for name, ref, start in ((FF, f, 0), (FL, f, width - size), (LF, l, 0), (LL, l, width - size)):
            put(member, name, ref[0, :, start : start + size], ref[1, :, start : start + size])
        put_coupling(member, coupling[0], coupling[1])
        for k in range(1, GROUP):
            mine, other = packs[2 * k - 2], packs[2 * k - 1]
            f, l = (mine, other) if first_is_own else (other, mine)
            slot = member ^ k
            put(slot, FF, f[0], f[1])
            put(slot, FL, f[2], f[3])
            put(slot, LF, l[0], l[1])
            put(slot, LL, l[2], l[3])
            put_coupling(slot, f[4], l[4])

    @pl.when(row == 0)
    def _():
        fill(True)

    @pl.when(row == 1)
    def _():
        fill(False)

    for k, v in enumerate(given):
        vectors[member ^ k] = v[...]
    first = [vectors[i, :half] for i in range(GROUP)]
    last = [vectors[i, half:].astype(F32) for i in range(GROUP)]
    unit = unit_columns(size)
    nothing = jnp.zeros_like(unit)

    def beside(x, below=nothing):
        return jnp.concatenate([x, below], axis=0)

    w = apply_short(maps[GROUP - 1, BN], unit)
    w = apply(maps[GROUP - 1, BN], apply_short(maps[GROUP - 1, LL], w), False)
    last_term[...] = w
    terms = [
        last[i] + apply(maps[i, LL], apply_short(maps[i, BN], first[i + 1]))
        for i in range(GROUP - 1)
    ] + [last[GROUP - 1]]
    u = beside(jnp.zeros((half, 2 * size), F32), unit)
    for i in range(GROUP):
        states[i] = u
        t = apply(maps[i, LF], u) + beside(terms[i])
        u = apply(maps[i, BN], t, False)
    leaving[...] = u
    s = apply(maps[GROUP - 1, FF], states[GROUP - 1]) + beside(first[GROUP - 1].astype(F32))
    backs[GROUP] = jnp.zeros_like(s)
    backs[GROUP - 1] = s
    for i in reversed(range(GROUP - 1)):
        e = apply(maps[i, FF], states[i]) + beside(first[i].astype(F32))
        s = e + apply(maps[i, FL], apply(maps[i, BN], s))
        backs[i] = s
    entering[...] = s
    left = slab < slabs // 2
    send[:half] = jnp.where(left, u[:half], s[:half]).astype(BF16)
    send[half : 2 * half] = first[0]
    send[2 * half :] = jnp.where(left, w, s[half:]).astype(BF16)
    here[...] = states[member]
    after[...] = backs[member + 1]


def gamma_kernel(maps, gamma, whole, backs):
    member = lax.axis_index("slab") % GROUP
    unit = unit_columns(gamma.shape[0])
    backs[GROUP] = unit
    s = apply(maps[GROUP - 1, FL], apply_short(maps[GROUP - 1, BN], unit))
    backs[GROUP - 1] = s
    for i in reversed(range(GROUP - 1)):
        s = apply(maps[i, FL], apply(maps[i, BN], s))
        backs[i] = s
    whole[...] = s
    gamma[...] = backs[member + 1]


def close_kernel(coupling, leaving, first, seen, last_term, here, after, gamma, out):
    half = first.shape[0]
    left = lax.axis_index("slab") < lax.axis_size("slab") // 2
    there = seen[:half].astype(F32)
    map_form = stacked(seen[2 * half :].astype(F32)).astype(BF16)
    b_re, b_im = coupling[0], coupling[1]
    b = jnp.concatenate(
        [jnp.concatenate([b_re, -b_im], axis=1), jnp.concatenate([b_im, b_re], axis=1)], axis=0
    )

    @pl.when(left)
    def _():
        ahead = seen[half : 2 * half].astype(F32)
        past = leaving[:half] + apply_computed(last_term[...], ahead)
        entry = there + apply(map_form, past, False)
        behind = after[:half] + apply_computed(gamma[...], entry)
        out[:half] = here[:half].astype(BF16)
        out[half:] = apply(b, behind).astype(BF16)

    @pl.when(jnp.logical_not(left))
    def _():
        before = there + apply_short(map_form, first[...], False)
        behind = after[:half] + apply_computed(after[half:], before)
        out[:half] = (here[:half] + apply_computed(here[half:], before)).astype(BF16)
        out[half:] = apply(b, behind).astype(BF16)


def final_kernel(count, green, direct, own, other, result, whole):
    row = lax.axis_index("row")
    shard_rows, width = green.shape[1:]
    half = own.shape[0] // 2
    columns = 2 * half
    surface = own.shape[1] // 2

    def place(first, second):
        for i in range(2):
            whole[i, :half] = first[i * half : (i + 1) * half]
            whole[i, half:] = second[i * half : (i + 1) * half]

    @pl.when(row == 0)
    def _():
        place(own, other)

    @pl.when(row == 1)
    def _():
        place(other, own)

    def product(start, x):
        g = jnp.concatenate(
            [green[0, :, start : start + surface], green[1, :, start : start + surface]], axis=1
        )
        x_re, x_im = x[:, :surface], x[:, surface:]
        form = jnp.concatenate(
            [jnp.concatenate([x_re, -x_im], axis=1), jnp.concatenate([x_im, x_re], axis=1)], axis=0
        )
        return contract(g, form, True)

    total = direct[...] + product(0, whole[0]) + product(width - surface, whole[1])
    orbital = row * shard_rows + lax.broadcasted_iota(jnp.int32, total.shape, 0)
    limit = jnp.concatenate([count[:1]] * (total.shape[1] // count.shape[1]), axis=1)
    live = (orbital < surface + limit) | (orbital >= width - surface)
    total = jnp.where(live, total, 0.0)
    result[0] = total[:, :columns]
    result[1] = total[:, columns:]


V, H = (pl.BlockSpec(memory_space=m) for m in (pltpu.VMEM, pltpu.HBM))


def call(kernel, specs, outs, scratch, *args, keep=False):
    args = [
        pltpu.with_memory_space_constraint(a, s.memory_space)
        for a, s in zip(args, specs, strict=True)
    ]
    kind = jax.ShapeDtypeStruct if keep else pltpu.VMEM
    return pl.pallas_call(
        kernel,
        in_specs=specs,
        out_specs=[V] * len(outs),
        out_shape=[kind(s, d) for s, d in outs],
        scratch_shapes=[pltpu.VMEM(*x) if isinstance(x, tuple) else x for x in scratch],
        compiler_params=pltpu.CompilerParams(vmem_limit_bytes=24 << 20),
    )(*args)


def compute(columns, x):
    size = columns.shape[1] // 2

    def mul(a, b):
        return jnp.dot(a, b, preferred_element_type=F32, precision=lax.Precision.HIGHEST)

    c_re, c_im = columns[:, :size], columns[:, size:]
    x_re, x_im = x[:, :size], x[:, size:]
    return jnp.concatenate([mul(x_re, c_re) - mul(x_im, c_im), mul(x_re, c_im) + mul(x_im, c_re)], axis=1)


def body(green_blocks, coupling, source, interior_count):
    shard_rows = green_blocks.shape[1]
    width = green_blocks.shape[2]
    surface = coupling.shape[1]
    columns = source.shape[2]
    half = columns // 2
    slab = lax.axis_index("slab")
    slabs = lax.axis_size("slab")

    def across(x):
        return lax.ppermute(x, "row", [(0, 1), (1, 0)])

    def partner(x, bit):
        return lax.ppermute(x, "slab", [(i, i ^ bit) for i in range(slabs)])

    square = (surface, 2 * surface)
    joint = (half + surface, 2 * surface)
    edge, pack, source_near = call(
        pack_kernel,
        [H] * 3,
        [
            ((2, surface, width), BF16),
            ((5, surface, surface), BF16),
            (source.shape, BF16),
        ],
        [pltpu.SemaphoreType.DMA((5,))],
        green_blocks,
        coupling,
        source,
    )
    count = jnp.broadcast_to(interior_count.reshape(1, 1), (8, columns))
    source_other = across(source_near)
    edge_other = across(edge)
    packs = [partner(pack, k) for k in range(1, GROUP)]
    (vectors,) = call(
        edge_kernel,
        [V] * 5,
        [((columns, 2 * surface), BF16)],
        [],
        count,
        edge,
        edge_other,
        source_near,
        source_other,
    )
    (direct,) = call(
        direct_kernel,
        [V] * 5,
        [((shard_rows, 2 * columns), F32)],
        [],
        count,
        green_blocks,
        source_near,
        source_other,
        vectors,
    )
    gathered = [partner(vectors, k) for k in range(1, GROUP)]
    both = []
    for p in packs:
        both += [p, across(p)]
    maps, send, here, after, last_term, leaving, entering = call(
        solve_kernel,
        [V] * (3 + len(both) + GROUP),
        [((GROUP, 5, 2 * surface, 2 * surface), BF16), ((columns + surface, 2 * surface), BF16)]
        + [(joint, F32)] * 2
        + [(square, F32)]
        + [(joint, F32)] * 2,
        [
            ((GROUP, columns, 2 * surface), BF16),
            ((GROUP,) + joint, F32),
            ((GROUP + 1,) + joint, F32),
        ],
        edge,
        edge_other,
        coupling,
        *both,
        vectors,
        *gathered,
    )
    gamma, back_whole = call(
        gamma_kernel, [V], [(square, F32), (square, F32)], [((GROUP + 1,) + square, F32)], maps
    )
    first = send[half:columns]
    bit = GROUP
    if 2 * bit < slabs:
        first = first.astype(F32)
        leave, a_map = leaving[:half], leaving[half:]
        back, d_map = entering[:half], entering[half:]
        pi, alpha, sigma, delta = here[:half], here[half:], after[:half], after[half:]
        c_map = back_whole
    while 2 * bit < slabs:
        right = (slab // bit) % 2 == 1

        def sides(own):
            seen = partner(own, bit)
            return jnp.where(right, seen, own), jnp.where(right, own, seen)

        (ax, ay), (cx, cy), (dx, dy) = sides(a_map), sides(c_map), sides(d_map)
        (wx, wy), (fx, fy) = sides(last_term), sides(first)
        (px, py), (qx, qy) = sides(leave), sides(back)
        middle = px + compute(wx, fy)
        entry = qy + compute(dy, middle)
        through = compute(dy, ax)
        pi = pi + jnp.where(right, compute(alpha, middle), 0.0)
        sigma = sigma + jnp.where(right, compute(delta, middle), compute(gamma, entry))
        delta = jnp.where(right, compute(delta, ax), delta + compute(gamma, through))
        alpha = jnp.where(right, compute(alpha, ax), alpha)
        gamma = jnp.where(right, gamma, compute(gamma, cy))
        leave, back = py + compute(ay, middle), qx + compute(cx, entry)
        a_map, c_map, d_map = compute(ay, ax), compute(cx, cy), dx + compute(cx, through)
        last_term, first = wy, fx
        bit *= 2
        if 2 * bit == slabs:
            left = slab < slabs // 2
            parts = [jnp.where(left, leave, back), first, jnp.where(left, last_term, d_map)]
            send = jnp.concatenate(parts, axis=0).astype(BF16)
            first = first.astype(BF16)
            leaving = jnp.concatenate([leave, a_map], axis=0)
            here = jnp.concatenate([pi, alpha], axis=0)
            after = jnp.concatenate([sigma, delta], axis=0)
    seen = partner(send, slabs // 2)
    (closed,) = call(
        close_kernel,
        [V] * 8,
        [((columns, 2 * surface), BF16)],
        [],
        coupling,
        leaving,
        first,
        seen,
        last_term,
        here,
        after,
        gamma,
    )
    (result,) = call(
        final_kernel,
        [V] * 5,
        [((2, shard_rows, columns), F32)],
        [((2, columns, 2 * surface), BF16)],
        count,
        green_blocks,
        direct,
        closed,
        across(closed),
        keep=True,
    )
    return result


def solution(mesh):
    placed = (
        P(None, ("energy", "slab", "row"), None),
        P(None, "slab", None),
        P(None, ("energy", "slab", "row"), None),
        P("slab"),
    )
    return jax.shard_map(
        body,
        mesh=mesh,
        in_specs=placed,
        out_specs=P(None, ("energy", "slab", "row"), None),
        check_vma=False,
    )
```

```python
import functools

import jax
import jax.numpy as jnp
from jax import lax
from jax.experimental import pallas as pl
from jax.experimental.pallas import tpu as pltpu
from jax.sharding import PartitionSpec as P


F32 = jnp.float32
BF16 = jnp.bfloat16
GROUP = 4
ORDER = (2, 1, 3)


def contract(x, matrix, across):
    return lax.dot_general(
        x, matrix, (((1,), (1 if across else 0,)), ((), ())), preferred_element_type=F32
    )


def split(x):
    high = x.astype(BF16)
    return high, (x - high.astype(F32)).astype(BF16)


def apply(real_form, x, across=True):
    high, low = split(x)
    both = contract(jnp.concatenate([high, low], axis=0), real_form, across)
    return both[: x.shape[0]] + both[x.shape[0] :]


def apply_short(real_form, x, across=True):
    return contract(x.astype(BF16), real_form, across)


def turned(x):
    half = x.shape[1] // 2
    return jnp.concatenate([-x[:, half:], x[:, :half]], axis=1)


def stacked(x):
    return jnp.concatenate([x, turned(x)], axis=0)


def apply_computed(columns, x):
    high, low = split(stacked(columns))
    x_high, x_low = split(x)
    both = contract(jnp.concatenate([x_high, x_low], axis=0), high, False)
    return both[: x.shape[0]] + both[x.shape[0] :] + contract(x_high, low, False)


def pack_kernel(green, coupling, source, edge, pack, source_near, couple_near, sems):
    row = lax.axis_index("row")
    shard_rows, width = green.shape[1:]
    surface = edge.shape[1]
    rows = pl.ds(pl.multiple_of(row * (shard_rows - surface), surface), surface)
    last = pl.ds(width - surface, surface)
    copies = [
        pltpu.make_async_copy(green.at[:, rows, pl.ds(0, surface)], pack.at[pl.ds(0, 2)], sems.at[0]),
        pltpu.make_async_copy(green.at[:, rows, last], pack.at[pl.ds(2, 2)], sems.at[1]),
        pltpu.make_async_copy(coupling.at[pl.ds(row, 1)], pack.at[pl.ds(4, 1)], sems.at[2]),
        pltpu.make_async_copy(green.at[:, rows], edge, sems.at[3]),
        pltpu.make_async_copy(source, source_near, sems.at[4]),
        pltpu.make_async_copy(coupling, couple_near, sems.at[5]),
    ]
    for c in copies:
        c.start()
    for c in copies:
        c.wait()


def masked_source(count, own, other, surface):
    row = lax.axis_index("row")
    orbitals = 2 * own.shape[1]

    def masked(part):
        mine, theirs = own[part].astype(F32), other[part].astype(F32)
        whole = jnp.concatenate(
            [jnp.where(row == 0, mine, theirs), jnp.where(row == 0, theirs, mine)], axis=0
        )
        orbital = lax.broadcasted_iota(jnp.int32, whole.shape, 0)
        live = (orbital < surface + count[:1]) | (orbital >= orbitals - surface)
        return jnp.where(live, whole, 0.0)

    real, imag = masked(0), masked(1)
    return (
        jnp.concatenate([real, imag], axis=1).astype(BF16),
        jnp.concatenate([-imag, real], axis=1).astype(BF16),
    )


def edge_kernel(count, edge, edge_other, source_own, source_other, vectors):
    row = lax.axis_index("row")
    surface = edge.shape[1]
    columns = source_own.shape[2]
    half = columns // 2
    above, below = masked_source(count, source_own, source_other, surface)

    def surface_rows(blocks):
        x = contract(blocks[0], above, False) + contract(blocks[1], below, False)
        whole = jnp.concatenate([x[:, :columns].T, x[:, columns:].T], axis=1)
        return jnp.where(row == 0, whole[:half], whole[half:]).astype(BF16)

    own, other = surface_rows(edge), surface_rows(edge_other)

    @pl.when(row == 0)
    def _():
        vectors[:half] = own
        vectors[half:] = other

    @pl.when(row == 1)
    def _():
        vectors[:half] = other
        vectors[half:] = own


def direct_kernel(count, green, source_own, source_other, surfaces, direct):
    above, below = masked_source(count, source_own, source_other, surfaces.shape[1] // 2)
    direct[...] = contract(green[0], above, False) + contract(green[1], below, False)


def unit_columns(size):
    eye = (
        lax.broadcasted_iota(jnp.int32, (size, size), 0)
        == lax.broadcasted_iota(jnp.int32, (size, size), 1)
    ).astype(F32)
    return jnp.concatenate([eye, jnp.zeros_like(eye)], axis=1)


NEAR, COUPLE, ALONG, BACK, SHIFT = 0, 1, 2, 4, 6


def apply_pair(x, forms, index, name):
    high, low = split(x)
    both = contract(jnp.concatenate([high, low], axis=0), forms[index, name], False)
    rest = contract(high, forms[index, name + 1], False)
    return both[: x.shape[0]] + both[x.shape[0] :] + rest


def columns_of(forms, index, name):
    size = forms.shape[2] // 2
    return forms[index, name, :size].astype(F32) + forms[index, name + 1, :size].astype(F32)


def real_form(re, im):
    return jnp.concatenate(
        [jnp.concatenate([re, -im], axis=1), jnp.concatenate([im, re], axis=1)], axis=0
    )


def form_slab(forms, k, near, far_first, far_last, along, b):
    slab = lax.axis_index("slab")
    slabs = lax.axis_size("slab")
    member = slab % GROUP
    known = slab - member + (member ^ k) < slabs - 1
    b_re, b_im = (jnp.where(known, x, jnp.zeros_like(x)) for x in b)
    couple = real_form(b_re, b_im)
    forms[k, NEAR] = real_form(*near)
    forms[k, COUPLE] = couple

    def transposed(re, im):
        return jnp.concatenate([re.astype(F32).T, im.astype(F32).T], axis=1).astype(BF16)

    def keep(name, x):
        high, low = split(stacked(x))
        forms[k, name] = high
        forms[k, name + 1] = low

    b_columns = transposed(b_re, b_im)
    keep(ALONG, contract(transposed(*along), couple, False))
    keep(BACK, contract(b_columns, real_form(*far_first), True))
    keep(SHIFT, apply(couple, contract(b_columns, real_form(*far_last), True), False))


def form_kernel(order, *refs):
    edge, edge_other, coupling = refs[:3]
    packs, forms = refs[3:-1], refs[-1]
    row = lax.axis_index("row")
    size = coupling.shape[1]
    width = edge.shape[2]

    def fill(first_is_own):
        f, l = (edge, edge_other) if first_is_own else (edge_other, edge)

        def corner(ref, start):
            return ref[0, :, start : start + size], ref[1, :, start : start + size]

        last = width - size
        form_slab(
            forms,
            0,
            corner(f, 0),
            corner(f, last),
            corner(l, last),
            corner(l, 0),
            (coupling[0], coupling[1]),
        )
        for n, k in enumerate(order):
            form_packed(forms, k, packs[2 * n], packs[2 * n + 1], first_is_own)

    @pl.when(row == 0)
    def _():
        fill(True)

    @pl.when(row == 1)
    def _():
        fill(False)


def form_packed(forms, k, mine, other, first_is_own):
    f, l = (mine, other) if first_is_own else (other, mine)
    form_slab(forms, k, (f[0], f[1]), (f[2], f[3]), (l[2], l[3]), (l[0], l[1]), (f[4], l[4]))


def response_kernel(last_k, _, mine, other, forms, alpha, delta, shift, through, whole, states, backs):
    row = lax.axis_index("row")
    slabs = lax.axis_size("slab")
    member = lax.axis_index("slab") % GROUP

    @pl.when(row == 0)
    def _():
        form_packed(forms, last_k, mine, other, True)

    @pl.when(row == 1)
    def _():
        form_packed(forms, last_k, mine, other, False)

    unit = unit_columns(alpha.shape[0])
    states[0] = unit
    u = columns_of(forms, member, ALONG)
    states[1] = u
    for i in range(1, GROUP):
        if i < GROUP - 1 or 2 * GROUP < slabs:
            u = apply_pair(u, forms, member ^ i, ALONG)
        if i < GROUP - 1:
            states[i + 1] = u
    through[...] = u
    backs[GROUP] = jnp.zeros_like(unit)
    s = apply(forms[member ^ (GROUP - 1), NEAR], states[GROUP - 1])
    backs[GROUP - 1] = s
    for i in reversed(range(GROUP - 1)):
        near = forms[member ^ i, NEAR]
        e = apply(near, states[i]) if i else apply_short(near, unit)
        s = e + apply_pair(s, forms, member ^ i, BACK)
        backs[i] = s
    whole[...] = s
    shift[...] = columns_of(forms, member ^ (GROUP - 1), SHIFT)
    alpha[...] = states[member]
    delta[...] = backs[member + 1]


def sweep_kernel(
    forms, shift, whole, v0, v1, v2, v3, send, leaving, entering, pi, sigma, vectors, states, backs
):
    slab = lax.axis_index("slab")
    member = slab % GROUP
    half = pi.shape[0]
    for k, v in enumerate((v0, v1, v2, v3)):
        vectors[member ^ k] = v[...]
    first = [vectors[i, :half] for i in range(GROUP)]
    terms = []
    for i in range(GROUP):
        term = contract(vectors[i, half:], forms[member ^ i, COUPLE], False)
        if i < GROUP - 1:
            term = term + contract(first[i + 1], forms[member ^ i, SHIFT], False)
            term = term + contract(first[i + 1], forms[member ^ i, SHIFT + 1], False)
        terms.append(term)
    states[0] = jnp.zeros(pi.shape, F32)
    u = terms[0]
    for i in range(1, GROUP):
        states[i] = u
        u = apply_pair(u, forms, member ^ i, ALONG) + terms[i]
    leaving[...] = u
    backs[GROUP] = jnp.zeros(pi.shape, F32)
    s = apply(forms[member ^ (GROUP - 1), NEAR], states[GROUP - 1]) + first[GROUP - 1].astype(F32)
    backs[GROUP - 1] = s
    for i in reversed(range(GROUP - 1)):
        e = first[i].astype(F32)
        if i:
            e = e + apply(forms[member ^ i, NEAR], states[i])
        s = e + apply_pair(s, forms, member ^ i, BACK)
        backs[i] = s
    entering[...] = s
    left = slab < lax.axis_size("slab") // 2
    send[:half] = jnp.where(left, u, s).astype(BF16)
    send[half : 2 * half] = first[0]
    send[2 * half :] = jnp.where(left, shift[...], whole[...]).astype(BF16)
    pi[...] = states[member]
    sigma[...] = backs[member + 1]


def gamma_kernel(forms, gamma, whole, backs):
    member = lax.axis_index("slab") % GROUP
    backs[GROUP] = unit_columns(gamma.shape[0])
    s = columns_of(forms, member ^ (GROUP - 1), BACK)
    backs[GROUP - 1] = s
    for i in reversed(range(GROUP - 1)):
        s = apply_pair(s, forms, member ^ i, BACK)
        backs[i] = s
    whole[...] = s
    gamma[...] = backs[member + 1]


def close_kernel(coupling, leaving, first, seen, shift, pi, sigma, alpha, delta, gamma, out):
    half = first.shape[0]
    left = lax.axis_index("slab") < lax.axis_size("slab") // 2
    there = seen[:half].astype(F32)
    map_form = stacked(seen[2 * half :].astype(F32)).astype(BF16)
    b = real_form(coupling[0], coupling[1])

    @pl.when(left)
    def _():
        ahead = seen[half : 2 * half].astype(F32)
        past = leaving[...] + apply_computed(shift[...], ahead)
        entry = there + apply(map_form, past, False)
        behind = sigma[...] + apply_computed(gamma[...], entry)
        out[:half] = pi[...].astype(BF16)
        out[half:] = apply(b, behind).astype(BF16)

    @pl.when(jnp.logical_not(left))
    def _():
        before = there + apply_short(map_form, first[...], False)
        behind = sigma[...] + apply_computed(delta[...], before)
        out[:half] = (pi[...] + apply_computed(alpha[...], before)).astype(BF16)
        out[half:] = apply(b, behind).astype(BF16)


def final_kernel(count, green, direct, own, other, result, whole):
    row = lax.axis_index("row")
    shard_rows, width = green.shape[1:]
    half = own.shape[0] // 2
    columns = 2 * half
    surface = own.shape[1] // 2

    def place(first, second):
        for i in range(2):
            whole[i, :half] = first[i * half : (i + 1) * half]
            whole[i, half:] = second[i * half : (i + 1) * half]

    @pl.when(row == 0)
    def _():
        place(own, other)

    @pl.when(row == 1)
    def _():
        place(other, own)

    def product(start, x):
        g = jnp.concatenate(
            [green[0, :, start : start + surface], green[1, :, start : start + surface]], axis=1
        )
        x_re, x_im = x[:, :surface], x[:, surface:]
        return contract(g, real_form(x_re, x_im), True)

    total = direct[...] + product(0, whole[0]) + product(width - surface, whole[1])
    orbital = row * shard_rows + lax.broadcasted_iota(jnp.int32, total.shape, 0)
    limit = jnp.concatenate([count[:1]] * (total.shape[1] // count.shape[1]), axis=1)
    live = (orbital < surface + limit) | (orbital >= width - surface)
    total = jnp.where(live, total, 0.0)
    result[0] = total[:, :columns]
    result[1] = total[:, columns:]


V, H = (pl.BlockSpec(memory_space=m) for m in (pltpu.VMEM, pltpu.HBM))


def call(kernel, specs, outs, scratch, *args, keep=False, aliases={}):
    args = [
        pltpu.with_memory_space_constraint(a, s.memory_space)
        for a, s in zip(args, specs, strict=True)
    ]
    kind = jax.ShapeDtypeStruct if keep else pltpu.VMEM
    return pl.pallas_call(
        kernel,
        in_specs=specs,
        out_specs=[V] * len(outs),
        out_shape=[kind(s, d) for s, d in outs],
        scratch_shapes=[pltpu.VMEM(*x) if isinstance(x, tuple) else x for x in scratch],
        input_output_aliases=aliases,
        compiler_params=pltpu.CompilerParams(vmem_limit_bytes=24 << 20),
    )(*args)


def compute(columns, x):
    size = columns.shape[1] // 2

    def mul(a, b):
        return jnp.dot(a, b, preferred_element_type=F32, precision=lax.Precision.HIGHEST)

    c_re, c_im = columns[:, :size], columns[:, size:]
    x_re, x_im = x[:, :size], x[:, size:]
    return jnp.concatenate([mul(x_re, c_re) - mul(x_im, c_im), mul(x_re, c_im) + mul(x_im, c_re)], axis=1)


def body(green_blocks, coupling, source, interior_count):
    shard_rows = green_blocks.shape[1]
    width = green_blocks.shape[2]
    surface = coupling.shape[1]
    columns = source.shape[2]
    half = columns // 2
    slab = lax.axis_index("slab")
    slabs = lax.axis_size("slab")

    def across(x):
        return lax.ppermute(x, "row", [(0, 1), (1, 0)])

    def partner(x, bit):
        return lax.ppermute(x, "slab", [(i, i ^ bit) for i in range(slabs)])

    square = (surface, 2 * surface)
    thin = (half, 2 * surface)
    edge, pack, source_near, couple_near = call(
        pack_kernel,
        [H] * 3,
        [
            ((2, surface, width), BF16),
            ((5, surface, surface), BF16),
            (source.shape, BF16),
            (coupling.shape, BF16),
        ],
        [pltpu.SemaphoreType.DMA((6,))],
        green_blocks,
        coupling,
        source,
    )
    count = jnp.broadcast_to(interior_count.reshape(1, 1), (8, columns))
    source_other = across(source_near)
    edge_other = across(edge)
    packs = {}
    for k in ORDER:
        packs[k] = partner(pack, k)
    (vectors,) = call(
        edge_kernel,
        [V] * 5,
        [((columns, 2 * surface), BF16)],
        [],
        count,
        edge,
        edge_other,
        source_near,
        source_other,
    )
    (direct,) = call(
        direct_kernel,
        [V] * 5,
        [((shard_rows, 2 * columns), F32)],
        [],
        count,
        green_blocks,
        source_near,
        source_other,
        vectors,
    )
    gathered = []
    for k in range(1, GROUP):
        gathered.append(partner(vectors, k))
    swapped = {}
    for k in ORDER:
        swapped[k] = across(packs[k])
    both = [x for k in ORDER[:-1] for x in (packs[k], swapped[k])]
    forms_shape = ((GROUP, 8, 2 * surface, 2 * surface), BF16)
    (forms,) = call(
        functools.partial(form_kernel, ORDER[:-1]),
        [V] * (3 + len(both)),
        [forms_shape],
        [],
        edge,
        edge_other,
        couple_near,
        *both,
    )
    forms, alpha, delta, shift, through, whole = call(
        functools.partial(response_kernel, ORDER[-1]),
        [V] * 3,
        [forms_shape] + [(square, F32)] * 5,
        [((GROUP,) + square, F32), ((GROUP + 1,) + square, F32)],
        forms,
        packs[ORDER[-1]],
        swapped[ORDER[-1]],
        aliases={0: 0},
    )
    send, leaving, entering, pi, sigma = call(
        sweep_kernel,
        [V] * (3 + GROUP),
        [((columns + surface, 2 * surface), BF16)] + [(thin, F32)] * 4,
        [((GROUP, columns, 2 * surface), BF16), ((GROUP,) + thin, F32), ((GROUP + 1,) + thin, F32)],
        forms,
        shift,
        whole,
        vectors,
        *gathered,
    )
    gamma, back_whole = call(
        gamma_kernel, [V], [(square, F32), (square, F32)], [((GROUP + 1,) + square, F32)], forms
    )
    first = send[half:columns]
    bit = GROUP
    if 2 * bit < slabs:
        first = first.astype(F32)
        a_map, d_map, c_map = through, whole, back_whole
    while 2 * bit < slabs:
        right = (slab // bit) % 2 == 1

        def sides(own):
            seen = partner(own, bit)
            return jnp.where(right, seen, own), jnp.where(right, own, seen)

        (ax, ay), (cx, cy), (dx, dy) = sides(a_map), sides(c_map), sides(d_map)
        (wx, wy), (fx, fy) = sides(shift), sides(first)
        (px, py), (qx, qy) = sides(leaving), sides(entering)
        middle = px + compute(wx, fy)
        entry = qy + compute(dy, middle)
        carried = compute(dy, ax)
        pi = pi + jnp.where(right, compute(alpha, middle), 0.0)
        sigma = sigma + jnp.where(right, compute(delta, middle), compute(gamma, entry))
        delta = jnp.where(right, compute(delta, ax), delta + compute(gamma, carried))
        alpha = jnp.where(right, compute(alpha, ax), alpha)
        gamma = jnp.where(right, gamma, compute(gamma, cy))
        leaving, entering = py + compute(ay, middle), qx + compute(cx, entry)
        a_map, c_map, d_map = compute(ay, ax), compute(cx, cy), dx + compute(cx, carried)
        shift, first = wy, fx
        bit *= 2
        if 2 * bit == slabs:
            left = slab < slabs // 2
            parts = [jnp.where(left, leaving, entering), first, jnp.where(left, shift, d_map)]
            send = jnp.concatenate(parts, axis=0).astype(BF16)
            first = first.astype(BF16)
    seen = partner(send, slabs // 2)
    (closed,) = call(
        close_kernel,
        [V] * 10,
        [((columns, 2 * surface), BF16)],
        [],
        couple_near,
        leaving,
        first,
        seen,
        shift,
        pi,
        sigma,
        alpha,
        delta,
        gamma,
    )
    (result,) = call(
        final_kernel,
        [V] * 5,
        [((2, shard_rows, columns), F32)],
        [((2, columns, 2 * surface), BF16)],
        count,
        green_blocks,
        direct,
        closed,
        across(closed),
        keep=True,
    )
    return result


def solution(mesh):
    placed = (
        P(None, ("energy", "slab", "row"), None),
        P(None, "slab", None),
        P(None, ("energy", "slab", "row"), None),
        P("slab"),
    )
    return jax.shard_map(
        body,
        mesh=mesh,
        in_specs=placed,
        out_specs=P(None, ("energy", "slab", "row"), None),
        check_vma=False,
    )
```

```python
import functools

import jax
import jax.numpy as jnp
from jax import lax
from jax.experimental import pallas as pl
from jax.experimental.pallas import tpu as pltpu
from jax.sharding import PartitionSpec as P


F32 = jnp.float32
BF16 = jnp.bfloat16
GROUP = 4
ORDER = (3, 1, 2)


def contract(x, matrix, across):
    return lax.dot_general(
        x, matrix, (((1,), (1 if across else 0,)), ((), ())), preferred_element_type=F32
    )


def split(x):
    high = x.astype(BF16)
    return high, (x - high.astype(F32)).astype(BF16)


def apply(real_form, x, across=True):
    high, low = split(x)
    both = contract(jnp.concatenate([high, low], axis=0), real_form, across)
    return both[: x.shape[0]] + both[x.shape[0] :]


def apply_short(real_form, x, across=True):
    return contract(x.astype(BF16), real_form, across)


def turned(x):
    half = x.shape[1] // 2
    return jnp.concatenate([-x[:, half:], x[:, :half]], axis=1)


def stacked(x):
    return jnp.concatenate([x, turned(x)], axis=0)


def apply_computed(columns, x):
    high, low = split(stacked(columns))
    x_high, x_low = split(x)
    both = contract(jnp.concatenate([x_high, x_low], axis=0), high, False)
    return both[: x.shape[0]] + both[x.shape[0] :] + contract(x_high, low, False)


def pack_kernel(green, coupling, source, edge, pack, source_near, couple_near, sems):
    row = lax.axis_index("row")
    shard_rows, width = green.shape[1:]
    surface = edge.shape[1]
    rows = pl.ds(pl.multiple_of(row * (shard_rows - surface), surface), surface)
    last = pl.ds(width - surface, surface)
    copies = [
        pltpu.make_async_copy(green.at[:, rows, pl.ds(0, surface)], pack.at[pl.ds(0, 2)], sems.at[0]),
        pltpu.make_async_copy(green.at[:, rows, last], pack.at[pl.ds(2, 2)], sems.at[1]),
        pltpu.make_async_copy(coupling.at[pl.ds(row, 1)], pack.at[pl.ds(4, 1)], sems.at[2]),
        pltpu.make_async_copy(green.at[:, rows], edge, sems.at[3]),
        pltpu.make_async_copy(source, source_near, sems.at[4]),
        pltpu.make_async_copy(coupling, couple_near, sems.at[5]),
    ]
    for c in copies:
        c.start()
    for c in copies:
        c.wait()


def masked_source(count, own, other, surface):
    row = lax.axis_index("row")
    orbitals = 2 * own.shape[1]

    def masked(part):
        mine, theirs = own[part].astype(F32), other[part].astype(F32)
        whole = jnp.concatenate(
            [jnp.where(row == 0, mine, theirs), jnp.where(row == 0, theirs, mine)], axis=0
        )
        orbital = lax.broadcasted_iota(jnp.int32, whole.shape, 0)
        live = (orbital < surface + count[:1]) | (orbital >= orbitals - surface)
        return jnp.where(live, whole, 0.0)

    real, imag = masked(0), masked(1)
    return (
        jnp.concatenate([real, imag], axis=1).astype(BF16),
        jnp.concatenate([-imag, real], axis=1).astype(BF16),
    )


def edge_kernel(count, edge, edge_other, source_own, source_other, vectors):
    row = lax.axis_index("row")
    surface = edge.shape[1]
    columns = source_own.shape[2]
    half = columns // 2
    above, below = masked_source(count, source_own, source_other, surface)

    def surface_rows(blocks):
        x = contract(blocks[0], above, False) + contract(blocks[1], below, False)
        whole = jnp.concatenate([x[:, :columns].T, x[:, columns:].T], axis=1)
        return jnp.where(row == 0, whole[:half], whole[half:]).astype(BF16)

    own, other = surface_rows(edge), surface_rows(edge_other)

    @pl.when(row == 0)
    def _():
        vectors[:half] = own
        vectors[half:] = other

    @pl.when(row == 1)
    def _():
        vectors[:half] = other
        vectors[half:] = own


def direct_kernel(count, green, source_own, source_other, surfaces, direct):
    above, below = masked_source(count, source_own, source_other, surfaces.shape[1] // 2)
    direct[...] = contract(green[0], above, False) + contract(green[1], below, False)


def unit_columns(size):
    eye = (
        lax.broadcasted_iota(jnp.int32, (size, size), 0)
        == lax.broadcasted_iota(jnp.int32, (size, size), 1)
    ).astype(F32)
    return jnp.concatenate([eye, jnp.zeros_like(eye)], axis=1)


NEAR, COUPLE, ALONG, BACK, SHIFT = 0, 1, 2, 4, 6


def apply_pair(x, forms, index, name):
    high, low = split(x)
    both = contract(jnp.concatenate([high, low], axis=0), forms[index, name], False)
    rest = contract(high, forms[index, name + 1], False)
    return both[: x.shape[0]] + both[x.shape[0] :] + rest


def columns_of(forms, index, name):
    size = forms.shape[2] // 2
    return forms[index, name, :size].astype(F32) + forms[index, name + 1, :size].astype(F32)


def real_form(re, im):
    return jnp.concatenate(
        [jnp.concatenate([re, -im], axis=1), jnp.concatenate([im, re], axis=1)], axis=0
    )


def form_slab(forms, k, near, far_first, far_last, along, b):
    slab = lax.axis_index("slab")
    slabs = lax.axis_size("slab")
    member = slab % GROUP
    known = slab - member + (member ^ k) < slabs - 1
    b_re, b_im = (jnp.where(known, x, jnp.zeros_like(x)) for x in b)
    couple = real_form(b_re, b_im)
    forms[k, NEAR] = real_form(*near)
    forms[k, COUPLE] = couple

    def transposed(re, im):
        return jnp.concatenate([re.astype(F32).T, im.astype(F32).T], axis=1).astype(BF16)

    def keep(name, x):
        high, low = split(stacked(x))
        forms[k, name] = high
        forms[k, name + 1] = low

    b_columns = transposed(b_re, b_im)
    keep(ALONG, contract(transposed(*along), couple, False))
    keep(BACK, contract(b_columns, real_form(*far_first), True))
    keep(SHIFT, apply(couple, contract(b_columns, real_form(*far_last), True), False))


def form_kernel(order, *refs):
    edge, edge_other, coupling = refs[:3]
    packs, forms = refs[3:-1], refs[-1]
    row = lax.axis_index("row")
    size = coupling.shape[1]
    width = edge.shape[2]

    def fill(first_is_own):
        f, l = (edge, edge_other) if first_is_own else (edge_other, edge)

        def corner(ref, start):
            return ref[0, :, start : start + size], ref[1, :, start : start + size]

        last = width - size
        form_slab(
            forms,
            0,
            corner(f, 0),
            corner(f, last),
            corner(l, last),
            corner(l, 0),
            (coupling[0], coupling[1]),
        )
        for n, k in enumerate(order):
            form_packed(forms, k, packs[2 * n], packs[2 * n + 1], first_is_own)

    @pl.when(row == 0)
    def _():
        fill(True)

    @pl.when(row == 1)
    def _():
        fill(False)


def form_packed(forms, k, mine, other, first_is_own):
    f, l = (mine, other) if first_is_own else (other, mine)
    form_slab(forms, k, (f[0], f[1]), (f[2], f[3]), (l[2], l[3]), (l[0], l[1]), (f[4], l[4]))


def solve_kernel(
    last_k, _, mine, other, v0, v1, v2, v3,
    forms, send, leaving, entering, here, after, shift, vectors, states, backs,
):
    row = lax.axis_index("row")
    slab = lax.axis_index("slab")
    slabs = lax.axis_size("slab")
    member = slab % GROUP
    size = shift.shape[0]
    half = vectors.shape[1] // 2

    @pl.when(row == 0)
    def _():
        form_packed(forms, last_k, mine, other, True)

    @pl.when(row == 1)
    def _():
        form_packed(forms, last_k, mine, other, False)

    for k, v in enumerate((v0, v1, v2, v3)):
        vectors[member ^ k] = v[...]
    first = [vectors[i, :half] for i in range(GROUP)]
    unit = unit_columns(size)
    nothing = jnp.zeros_like(unit)

    def beside(x, below=nothing):
        return jnp.concatenate([x, below], axis=0)

    terms = []
    for i in range(GROUP):
        term = contract(vectors[i, half:], forms[member ^ i, COUPLE], False)
        if i < GROUP - 1:
            term = term + contract(first[i + 1], forms[member ^ i, SHIFT], False)
            term = term + contract(first[i + 1], forms[member ^ i, SHIFT + 1], False)
        terms.append(term)
    states[0] = beside(jnp.zeros_like(terms[0]), unit)
    u = beside(terms[0], columns_of(forms, member, ALONG))
    for i in range(1, GROUP - 1):
        states[i] = u
        u = apply_pair(u, forms, member ^ i, ALONG) + beside(terms[i])
    states[GROUP - 1] = u
    last = member ^ (GROUP - 1)
    s = apply(forms[last, NEAR], u) + beside(first[GROUP - 1].astype(F32))
    if 2 * GROUP < slabs:
        u = apply_pair(u, forms, last, ALONG) + beside(terms[GROUP - 1])
        leaving[...] = u
    else:
        u = apply_pair(u[:half], forms, last, ALONG) + terms[GROUP - 1]
        leaving[:half] = u
        leaving[half:] = nothing
    backs[GROUP] = jnp.zeros_like(s)
    backs[GROUP - 1] = s
    for i in reversed(range(GROUP - 1)):
        near = forms[member ^ i, NEAR]
        if i:
            e = apply(near, states[i]) + beside(first[i].astype(F32))
        else:
            e = beside(first[i].astype(F32), apply_short(near, unit))
        s = e + apply_pair(s, forms, member ^ i, BACK)
        backs[i] = s
    entering[...] = s
    w = columns_of(forms, last, SHIFT)
    shift[...] = w
    left = slab < slabs // 2
    send[:half] = jnp.where(left, u[:half], s[:half]).astype(BF16)
    send[half : 2 * half] = first[0]
    send[2 * half :] = jnp.where(left, w, s[half:]).astype(BF16)
    here[...] = states[member]
    after[...] = backs[member + 1]


def gamma_kernel(forms, gamma, whole, backs):
    member = lax.axis_index("slab") % GROUP
    backs[GROUP] = unit_columns(gamma.shape[0])
    s = columns_of(forms, member ^ (GROUP - 1), BACK)
    backs[GROUP - 1] = s
    for i in reversed(range(GROUP - 1)):
        s = apply_pair(s, forms, member ^ i, BACK)
        backs[i] = s
    whole[...] = s
    gamma[...] = backs[member + 1]


def close_kernel(coupling, leaving, first, seen, shift, here, after, gamma, out):
    half = first.shape[0]
    left = lax.axis_index("slab") < lax.axis_size("slab") // 2
    there = seen[:half].astype(F32)
    map_form = stacked(seen[2 * half :].astype(F32)).astype(BF16)
    b = real_form(coupling[0], coupling[1])

    @pl.when(left)
    def _():
        ahead = seen[half : 2 * half].astype(F32)
        past = leaving[:half] + apply_computed(shift[...], ahead)
        entry = there + apply(map_form, past, False)
        behind = after[:half] + apply_computed(gamma[...], entry)
        out[:half] = here[:half].astype(BF16)
        out[half:] = apply(b, behind).astype(BF16)

    @pl.when(jnp.logical_not(left))
    def _():
        before = there + apply_short(map_form, first[...], False)
        behind = after[:half] + apply_computed(after[half:], before)
        out[:half] = (here[:half] + apply_computed(here[half:], before)).astype(BF16)
        out[half:] = apply(b, behind).astype(BF16)


def final_kernel(count, green, direct, own, other, result, whole):
    row = lax.axis_index("row")
    shard_rows, width = green.shape[1:]
    half = own.shape[0] // 2
    columns = 2 * half
    surface = own.shape[1] // 2

    def place(first, second):
        for i in range(2):
            whole[i, :half] = first[i * half : (i + 1) * half]
            whole[i, half:] = second[i * half : (i + 1) * half]

    @pl.when(row == 0)
    def _():
        place(own, other)

    @pl.when(row == 1)
    def _():
        place(other, own)

    def product(start, x):
        g = jnp.concatenate(
            [green[0, :, start : start + surface], green[1, :, start : start + surface]], axis=1
        )
        x_re, x_im = x[:, :surface], x[:, surface:]
        return contract(g, real_form(x_re, x_im), True)

    total = direct[...] + product(0, whole[0]) + product(width - surface, whole[1])
    orbital = row * shard_rows + lax.broadcasted_iota(jnp.int32, total.shape, 0)
    limit = jnp.concatenate([count[:1]] * (total.shape[1] // count.shape[1]), axis=1)
    live = (orbital < surface + limit) | (orbital >= width - surface)
    total = jnp.where(live, total, 0.0)
    result[0] = total[:, :columns]
    result[1] = total[:, columns:]


V, H = (pl.BlockSpec(memory_space=m) for m in (pltpu.VMEM, pltpu.HBM))


def call(kernel, specs, outs, scratch, *args, keep=False, aliases={}):
    args = [
        pltpu.with_memory_space_constraint(a, s.memory_space)
        for a, s in zip(args, specs, strict=True)
    ]
    kind = jax.ShapeDtypeStruct if keep else pltpu.VMEM
    return pl.pallas_call(
        kernel,
        in_specs=specs,
        out_specs=[V] * len(outs),
        out_shape=[kind(s, d) for s, d in outs],
        scratch_shapes=[pltpu.VMEM(*x) if isinstance(x, tuple) else x for x in scratch],
        input_output_aliases=aliases,
        compiler_params=pltpu.CompilerParams(vmem_limit_bytes=24 << 20),
    )(*args)


def compute(columns, x):
    size = columns.shape[1] // 2

    def mul(a, b):
        return jnp.dot(a, b, preferred_element_type=F32, precision=lax.Precision.HIGHEST)

    c_re, c_im = columns[:, :size], columns[:, size:]
    x_re, x_im = x[:, :size], x[:, size:]
    return jnp.concatenate([mul(x_re, c_re) - mul(x_im, c_im), mul(x_re, c_im) + mul(x_im, c_re)], axis=1)


def body(green_blocks, coupling, source, interior_count):
    shard_rows = green_blocks.shape[1]
    width = green_blocks.shape[2]
    surface = coupling.shape[1]
    columns = source.shape[2]
    half = columns // 2
    slab = lax.axis_index("slab")
    slabs = lax.axis_size("slab")

    def across(x):
        return lax.ppermute(x, "row", [(0, 1), (1, 0)])

    def partner(x, bit):
        return lax.ppermute(x, "slab", [(i, i ^ bit) for i in range(slabs)])

    square = (surface, 2 * surface)
    joint = (half + surface, 2 * surface)
    edge, pack, source_near, couple_near = call(
        pack_kernel,
        [H] * 3,
        [
            ((2, surface, width), BF16),
            ((5, surface, surface), BF16),
            (source.shape, BF16),
            (coupling.shape, BF16),
        ],
        [pltpu.SemaphoreType.DMA((6,))],
        green_blocks,
        coupling,
        source,
    )
    count = jnp.broadcast_to(interior_count.reshape(1, 1), (8, columns))
    source_other = across(source_near)
    edge_other = across(edge)
    packs = {}
    for k in ORDER:
        packs[k] = partner(pack, k)
    (vectors,) = call(
        edge_kernel,
        [V] * 5,
        [((columns, 2 * surface), BF16)],
        [],
        count,
        edge,
        edge_other,
        source_near,
        source_other,
    )
    (direct,) = call(
        direct_kernel,
        [V] * 5,
        [((shard_rows, 2 * columns), F32)],
        [],
        count,
        green_blocks,
        source_near,
        source_other,
        vectors,
    )
    gathered = []
    for k in range(1, GROUP):
        gathered.append(partner(vectors, k))
    swapped = {}
    for k in ORDER:
        swapped[k] = across(packs[k])
    both = [x for k in ORDER[:-1] for x in (packs[k], swapped[k])]
    forms_shape = ((GROUP, 8, 2 * surface, 2 * surface), BF16)
    (forms,) = call(
        functools.partial(form_kernel, ORDER[:-1]),
        [V] * (3 + len(both)),
        [forms_shape],
        [],
        edge,
        edge_other,
        couple_near,
        *both,
    )
    forms, send, leaving, entering, here, after, shift = call(
        functools.partial(solve_kernel, ORDER[-1]),
        [V] * (3 + GROUP),
        [forms_shape, ((columns + surface, 2 * surface), BF16)]
        + [(joint, F32)] * 4
        + [(square, F32)],
        [
            ((GROUP, columns, 2 * surface), BF16),
            ((GROUP,) + joint, F32),
            ((GROUP + 1,) + joint, F32),
        ],
        forms,
        packs[ORDER[-1]],
        swapped[ORDER[-1]],
        vectors,
        *gathered,
        aliases={0: 0},
    )
    gamma, back_whole = call(
        gamma_kernel, [V], [(square, F32), (square, F32)], [((GROUP + 1,) + square, F32)], forms
    )
    first = send[half:columns]
    bit = GROUP
    if 2 * bit < slabs:
        first = first.astype(F32)
        leave, a_map = leaving[:half], leaving[half:]
        back, d_map = entering[:half], entering[half:]
        pi, alpha, sigma, delta = here[:half], here[half:], after[:half], after[half:]
        c_map = back_whole
    while 2 * bit < slabs:
        right = (slab // bit) % 2 == 1

        def sides(own):
            seen = partner(own, bit)
            return jnp.where(right, seen, own), jnp.where(right, own, seen)

        (ax, ay), (cx, cy), (dx, dy) = sides(a_map), sides(c_map), sides(d_map)
        (wx, wy), (fx, fy) = sides(shift), sides(first)
        (px, py), (qx, qy) = sides(leave), sides(back)
        middle = px + compute(wx, fy)
        entry = qy + compute(dy, middle)
        carried = compute(dy, ax)
        pi = pi + jnp.where(right, compute(alpha, middle), 0.0)
        sigma = sigma + jnp.where(right, compute(delta, middle), compute(gamma, entry))
        delta = jnp.where(right, compute(delta, ax), delta + compute(gamma, carried))
        alpha = jnp.where(right, compute(alpha, ax), alpha)
        gamma = jnp.where(right, gamma, compute(gamma, cy))
        leave, back = py + compute(ay, middle), qx + compute(cx, entry)
        a_map, c_map, d_map = compute(ay, ax), compute(cx, cy), dx + compute(cx, carried)
        shift, first = wy, fx
        bit *= 2
        if 2 * bit == slabs:
            left = slab < slabs // 2
            parts = [jnp.where(left, leave, back), first, jnp.where(left, shift, d_map)]
            send = jnp.concatenate(parts, axis=0).astype(BF16)
            first = first.astype(BF16)
            leaving = jnp.concatenate([leave, a_map], axis=0)
            here = jnp.concatenate([pi, alpha], axis=0)
            after = jnp.concatenate([sigma, delta], axis=0)
    seen = partner(send, slabs // 2)
    (closed,) = call(
        close_kernel,
        [V] * 8,
        [((columns, 2 * surface), BF16)],
        [],
        couple_near,
        leaving,
        first,
        seen,
        shift,
        here,
        after,
        gamma,
    )
    (result,) = call(
        final_kernel,
        [V] * 5,
        [((2, shard_rows, columns), F32)],
        [((2, columns, 2 * surface), BF16)],
        count,
        green_blocks,
        direct,
        closed,
        across(closed),
        keep=True,
    )
    return result


def solution(mesh):
    placed = (
        P(None, ("energy", "slab", "row"), None),
        P(None, "slab", None),
        P(None, ("energy", "slab", "row"), None),
        P("slab"),
    )
    return jax.shard_map(
        body,
        mesh=mesh,
        in_specs=placed,
        out_specs=P(None, ("energy", "slab", "row"), None),
        check_vma=False,
    )
```

```python
import functools

import jax
import jax.numpy as jnp
from jax import lax
from jax.experimental import pallas as pl
from jax.experimental.pallas import tpu as pltpu
from jax.sharding import PartitionSpec as P


F32 = jnp.float32
BF16 = jnp.bfloat16
GROUP = 4
ORDER = (3, 2, 1)
EARLY = 2


def contract(x, matrix, across):
    return lax.dot_general(
        x, matrix, (((1,), (1 if across else 0,)), ((), ())), preferred_element_type=F32
    )


def split(x):
    high = x.astype(BF16)
    return high, (x - high.astype(F32)).astype(BF16)


def apply(real_form, x, across=True):
    high, low = split(x)
    both = contract(jnp.concatenate([high, low], axis=0), real_form, across)
    return both[: x.shape[0]] + both[x.shape[0] :]


def apply_short(real_form, x, across=True):
    return contract(x.astype(BF16), real_form, across)


def turned(x):
    half = x.shape[1] // 2
    return jnp.concatenate([-x[:, half:], x[:, :half]], axis=1)


def stacked(x):
    return jnp.concatenate([x, turned(x)], axis=0)


def run_copies(pairs, sems):
    copies = [pltpu.make_async_copy(a, b, sems.at[n]) for n, (a, b) in enumerate(pairs)]
    for c in copies:
        c.start()
    for c in copies:
        c.wait()


def own_rows(green, surface):
    row = lax.axis_index("row")
    return pl.ds(pl.multiple_of(row * (green.shape[1] - surface), surface), surface)


def pack_kernel(green, coupling, pack, sems):
    surface = pack.shape[1]
    rows = own_rows(green, surface)
    last = pl.ds(green.shape[2] - surface, surface)
    part = pl.ds(lax.axis_index("row"), 1)
    run_copies(
        [
            (green.at[:, rows, pl.ds(0, surface)], pack.at[pl.ds(0, 2)]),
            (green.at[:, rows, last], pack.at[pl.ds(2, 2)]),
            (coupling.at[part], pack.at[pl.ds(4, 1)]),
        ],
        sems,
    )


def near_kernel(green, coupling, source, pack, edge, source_near, couple_near, sems):
    rows = own_rows(green, edge.shape[1])
    run_copies(
        [(green.at[:, rows], edge), (source, source_near), (coupling, couple_near)], sems
    )


def masked_source(count, own, other, surface):
    row = lax.axis_index("row")
    orbitals = 2 * own.shape[1]

    def masked(part):
        mine, theirs = own[part].astype(F32), other[part].astype(F32)
        whole = jnp.concatenate(
            [jnp.where(row == 0, mine, theirs), jnp.where(row == 0, theirs, mine)], axis=0
        )
        orbital = lax.broadcasted_iota(jnp.int32, whole.shape, 0)
        live = (orbital < surface + count[:1]) | (orbital >= orbitals - surface)
        return jnp.where(live, whole, 0.0)

    real, imag = masked(0), masked(1)
    return (
        jnp.concatenate([real, imag], axis=1).astype(BF16),
        jnp.concatenate([-imag, real], axis=1).astype(BF16),
    )


def edge_kernel(count, edge, edge_other, source_own, source_other, vectors):
    row = lax.axis_index("row")
    surface = edge.shape[1]
    columns = source_own.shape[2]
    half = columns // 2
    above, below = masked_source(count, source_own, source_other, surface)

    def surface_rows(blocks):
        x = contract(blocks[0], above, False) + contract(blocks[1], below, False)
        whole = jnp.concatenate([x[:, :columns].T, x[:, columns:].T], axis=1)
        return jnp.where(row == 0, whole[:half], whole[half:]).astype(BF16)

    own, other = surface_rows(edge), surface_rows(edge_other)

    @pl.when(row == 0)
    def _():
        vectors[:half] = own
        vectors[half:] = other

    @pl.when(row == 1)
    def _():
        vectors[:half] = other
        vectors[half:] = own


def direct_kernel(count, green, source_own, source_other, surfaces, direct):
    above, below = masked_source(count, source_own, source_other, surfaces.shape[1] // 2)
    direct[...] = contract(green[0], above, False) + contract(green[1], below, False)


def unit_rows(start, count, size):
    eye = (
        start + lax.broadcasted_iota(jnp.int32, (count, size), 0)
        == lax.broadcasted_iota(jnp.int32, (count, size), 1)
    ).astype(F32)
    return jnp.concatenate([eye, jnp.zeros_like(eye)], axis=1)


NEAR, COUPLE, ALONG, BACK, SHIFT = 0, 1, 2, 4, 6


def apply_pair(x, forms, index, name):
    high, low = split(x)
    both = contract(jnp.concatenate([high, low], axis=0), forms[index, name], False)
    rest = contract(high, forms[index, name + 1], False)
    return both[: x.shape[0]] + both[x.shape[0] :] + rest


def columns_of(forms, index, name, rows=None):
    rows = pl.ds(0, forms.shape[2] // 2) if rows is None else rows
    return forms[index, name, rows].astype(F32) + forms[index, name + 1, rows].astype(F32)


def real_form(re, im):
    return jnp.concatenate(
        [jnp.concatenate([re, -im], axis=1), jnp.concatenate([im, re], axis=1)], axis=0
    )


def form_slab(forms, k, near, far_first, far_last, along, b):
    slab = lax.axis_index("slab")
    slabs = lax.axis_size("slab")
    member = slab % GROUP
    known = slab - member + (member ^ k) < slabs - 1
    b_re, b_im = (jnp.where(known, x, jnp.zeros_like(x)) for x in b)
    couple = real_form(b_re, b_im)
    forms[k, NEAR] = real_form(*near)
    forms[k, COUPLE] = couple

    def transposed(re, im):
        return jnp.concatenate([re.astype(F32).T, im.astype(F32).T], axis=1).astype(BF16)

    def keep(name, x):
        high, low = split(stacked(x))
        forms[k, name] = high
        forms[k, name + 1] = low

    b_columns = transposed(b_re, b_im)
    keep(ALONG, contract(transposed(*along), couple, False))
    keep(BACK, contract(b_columns, real_form(*far_first), True))
    keep(SHIFT, apply(couple, contract(b_columns, real_form(*far_last), True), False))


def form_kernel(order, *refs):
    edge, edge_other, coupling = refs[:3]
    packs, forms = refs[3:-1], refs[-1]
    row = lax.axis_index("row")
    size = coupling.shape[1]
    width = edge.shape[2]

    def fill(first_is_own):
        f, l = (edge, edge_other) if first_is_own else (edge_other, edge)

        def corner(ref, start):
            return ref[0, :, start : start + size], ref[1, :, start : start + size]

        last = width - size
        form_slab(
            forms,
            0,
            corner(f, 0),
            corner(f, last),
            corner(l, last),
            corner(l, 0),
            (coupling[0], coupling[1]),
        )
        for n, k in enumerate(order):
            form_packed(forms, k, packs[2 * n], packs[2 * n + 1], first_is_own)

    @pl.when(row == 0)
    def _():
        fill(True)

    @pl.when(row == 1)
    def _():
        fill(False)


def form_packed(forms, k, mine, other, first_is_own):
    f, l = (mine, other) if first_is_own else (other, mine)
    form_slab(forms, k, (f[0], f[1]), (f[2], f[3]), (l[2], l[3]), (l[0], l[1]), (f[4], l[4]))


def solve_kernel(
    later, _, *refs
):
    packed, given = refs[: 2 * len(later)], refs[2 * len(later) : 2 * len(later) + GROUP]
    forms, send, send_map, leaving, entering, pi, sigma, response, shift, vectors, states, backs = refs[
        2 * len(later) + GROUP :
    ]
    row = lax.axis_index("row")
    slab = lax.axis_index("slab")
    slabs = lax.axis_size("slab")
    member = slab % GROUP
    size = shift.shape[0]
    half = vectors.shape[1] // 2

    def fill(first_is_own):
        for n, k in enumerate(later):
            form_packed(forms, k, packed[2 * n], packed[2 * n + 1], first_is_own)

    @pl.when(row == 0)
    def _():
        fill(True)

    @pl.when(row == 1)
    def _():
        fill(False)

    for k, v in enumerate(given):
        vectors[member ^ k] = v[...]
    first = [vectors[i, :half] for i in range(GROUP)]
    rows = pl.ds(pl.multiple_of(row * half, half), half)
    unit = unit_rows(row * half, half, size)
    nothing = jnp.zeros_like(unit)

    def beside(x, below=nothing):
        return jnp.concatenate([x, below], axis=0)

    terms = []
    for i in range(GROUP):
        term = contract(vectors[i, half:], forms[member ^ i, COUPLE], False)
        if i < GROUP - 1:
            term = term + contract(first[i + 1], forms[member ^ i, SHIFT], False)
            term = term + contract(first[i + 1], forms[member ^ i, SHIFT + 1], False)
        terms.append(term)
    states[0] = beside(jnp.zeros_like(terms[0]), unit)
    u = beside(terms[0], columns_of(forms, member, ALONG, rows))
    for i in range(1, GROUP - 1):
        states[i] = u
        u = apply_pair(u, forms, member ^ i, ALONG) + beside(terms[i])
    states[GROUP - 1] = u
    last = member ^ (GROUP - 1)
    s = apply(forms[last, NEAR], u) + beside(first[GROUP - 1].astype(F32))
    if 2 * GROUP < slabs:
        u = apply_pair(u, forms, last, ALONG) + beside(terms[GROUP - 1])
        leaving[...] = u
    else:
        u = apply_pair(u[:half], forms, last, ALONG) + terms[GROUP - 1]
        leaving[:half] = u
        leaving[half:] = nothing
    backs[GROUP] = jnp.zeros_like(s)
    backs[GROUP - 1] = s
    for i in reversed(range(GROUP - 1)):
        near = forms[member ^ i, NEAR]
        if i:
            e = apply(near, states[i]) + beside(first[i].astype(F32))
        else:
            e = beside(first[i].astype(F32), apply_short(near, unit))
        s = e + apply_pair(s, forms, member ^ i, BACK)
        backs[i] = s
    entering[...] = s
    shift[...] = columns_of(forms, last, SHIFT)
    left = slab < slabs // 2
    send[:half] = jnp.where(left, u[:half], s[:half]).astype(BF16)
    send[half:] = first[0]
    send_map[...] = jnp.where(left, columns_of(forms, last, SHIFT, rows), s[half:]).astype(BF16)
    here, after = states[member], backs[member + 1]
    pi[...] = here[:half]
    sigma[...] = after[:half]
    response[:half] = here[half:]
    response[half:] = after[half:]


def gamma_kernel(forms, gamma, whole, backs):
    member = lax.axis_index("slab") % GROUP
    backs[GROUP] = unit_rows(0, gamma.shape[0], gamma.shape[0])
    s = columns_of(forms, member ^ (GROUP - 1), BACK)
    backs[GROUP - 1] = s
    for i in reversed(range(GROUP - 1)):
        s = apply_pair(s, forms, member ^ i, BACK)
        backs[i] = s
    whole[...] = s
    gamma[...] = backs[member + 1]


def ready_kernel(coupling, sigma, response, response_other, gamma, shift, hand, base, whole):
    row = lax.axis_index("row")
    half = base.shape[0]
    left = lax.axis_index("slab") < lax.axis_size("slab") // 2
    b = real_form(coupling[0], coupling[1])

    def place(first, second):
        for i in range(2):
            whole[i, :half] = first[i * half : (i + 1) * half]
            whole[i, half:] = second[i * half : (i + 1) * half]

    @pl.when(row == 0)
    def _():
        place(response, response_other)

    @pl.when(row == 1)
    def _():
        place(response_other, response)

    def keep(index, x):
        hand[index], hand[index + 1] = split(stacked(x))

    keep(0, jnp.where(left, shift[...], whole[0]))
    keep(2, apply(b, jnp.where(left, gamma[...], whole[1])))
    base[...] = apply(b, sigma[...])


def close_kernel(hand, base, pi, leaving, first, seen, map_seen, map_other, out, rows):
    row = lax.axis_index("row")
    half = first.shape[0]
    part = map_seen.shape[0]
    left = lax.axis_index("slab") < lax.axis_size("slab") // 2
    there = seen[:half].astype(F32)

    @pl.when(row == 0)
    def _():
        rows[:part] = map_seen[...]
        rows[part:] = map_other[...]

    @pl.when(row == 1)
    def _():
        rows[:part] = map_other[...]
        rows[part:] = map_seen[...]

    map_form = stacked(rows[...])

    def times(x, index):
        high, low = split(x)
        both = contract(jnp.concatenate([high, low], axis=0), hand[index], False)
        return both[:half] + both[half:] + contract(high, hand[index + 1], False)

    @pl.when(left)
    def _():
        ahead = seen[half:]
        past = leaving[:half] + contract(ahead, hand[0], False) + contract(ahead, hand[1], False)
        entry = there + apply(map_form, past, False)
        out[:half] = pi[...].astype(BF16)
        out[half:] = (base[...] + times(entry, 2)).astype(BF16)

    @pl.when(jnp.logical_not(left))
    def _():
        before = there + apply_short(map_form, first[...], False)
        out[:half] = (pi[...] + times(before, 0)).astype(BF16)
        out[half:] = (base[...] + times(before, 2)).astype(BF16)


def final_kernel(count, green, direct, own, other, result, whole):
    row = lax.axis_index("row")
    shard_rows, width = green.shape[1:]
    half = own.shape[0] // 2
    columns = 2 * half
    surface = own.shape[1] // 2

    def place(first, second):
        for i in range(2):
            whole[i, :half] = first[i * half : (i + 1) * half]
            whole[i, half:] = second[i * half : (i + 1) * half]

    @pl.when(row == 0)
    def _():
        place(own, other)

    @pl.when(row == 1)
    def _():
        place(other, own)

    total = direct[...]
    for start, x in ((0, whole[0]), (width - surface, whole[1])):
        cols = slice(start, start + surface)
        g = jnp.concatenate([green[0, :, cols], green[1, :, cols]], axis=1)
        total = total + contract(g, real_form(x[:, :surface], x[:, surface:]), True)
    orbital = row * shard_rows + lax.broadcasted_iota(jnp.int32, total.shape, 0)
    limit = jnp.concatenate([count[:1]] * (total.shape[1] // count.shape[1]), axis=1)
    live = (orbital < surface + limit) | (orbital >= width - surface)
    total = jnp.where(live, total, 0.0)
    result[0] = total[:, :columns]
    result[1] = total[:, columns:]


V, H = (pl.BlockSpec(memory_space=m) for m in (pltpu.VMEM, pltpu.HBM))


def call(kernel, specs, outs, scratch, *args, keep=False, aliases={}):
    args = [
        pltpu.with_memory_space_constraint(a, s.memory_space)
        for a, s in zip(args, specs, strict=True)
    ]
    kind = jax.ShapeDtypeStruct if keep else pltpu.VMEM
    return pl.pallas_call(
        kernel,
        in_specs=specs,
        out_specs=[V] * len(outs),
        out_shape=[kind(s, d) for s, d in outs],
        scratch_shapes=[pltpu.VMEM(*x) if isinstance(x, tuple) else x for x in scratch],
        input_output_aliases=aliases,
        compiler_params=pltpu.CompilerParams(vmem_limit_bytes=24 << 20),
    )(*args)


def compute(columns, x):
    size = columns.shape[1] // 2

    def mul(a, b):
        return jnp.dot(a, b, preferred_element_type=F32, precision=lax.Precision.HIGHEST)

    c_re, c_im = columns[:, :size], columns[:, size:]
    x_re, x_im = x[:, :size], x[:, size:]
    return jnp.concatenate([mul(x_re, c_re) - mul(x_im, c_im), mul(x_re, c_im) + mul(x_im, c_re)], axis=1)


def body(green_blocks, coupling, source, interior_count):
    shard_rows = green_blocks.shape[1]
    width = green_blocks.shape[2]
    surface = coupling.shape[1]
    columns = source.shape[2]
    half = columns // 2
    slab = lax.axis_index("slab")
    slabs = lax.axis_size("slab")

    def across(x):
        return lax.ppermute(x, "row", [(0, 1), (1, 0)])

    def partner(x, bit):
        return lax.ppermute(x, "slab", [(i, i ^ bit) for i in range(slabs)])

    square = (surface, 2 * surface)
    thin, joint = (half, 2 * surface), (columns, 2 * surface)
    (pack,) = call(
        pack_kernel,
        [H] * 2,
        [((5, surface, surface), BF16)],
        [pltpu.SemaphoreType.DMA((3,))],
        green_blocks,
        coupling,
    )
    edge, source_near, couple_near = call(
        near_kernel,
        [H] * 3 + [V],
        [((2, surface, width), BF16), (source.shape, BF16), (coupling.shape, BF16)],
        [pltpu.SemaphoreType.DMA((3,))],
        green_blocks,
        coupling,
        source,
        pack,
    )
    count = jnp.broadcast_to(interior_count.reshape(1, 1), (8, columns))
    source_other = across(source_near)
    edge_other = across(edge)
    packs = {}
    for k in ORDER:
        packs[k] = partner(pack, k)
    (vectors,) = call(
        edge_kernel,
        [V] * 5,
        [((columns, 2 * surface), BF16)],
        [],
        count,
        edge,
        edge_other,
        source_near,
        source_other,
    )
    (direct,) = call(
        direct_kernel,
        [V] * 5,
        [((shard_rows, 2 * columns), F32)],
        [],
        count,
        green_blocks,
        source_near,
        source_other,
        vectors,
    )
    gathered = []
    for k in range(1, GROUP):
        gathered.append(partner(vectors, k))
    swapped = {}
    for k in ORDER:
        swapped[k] = across(packs[k])
    sooner, later = ORDER[:EARLY], ORDER[EARLY:]
    forms_shape = ((GROUP, 8, 2 * surface, 2 * surface), BF16)
    (forms,) = call(
        functools.partial(form_kernel, sooner),
        [V] * (3 + 2 * len(sooner)),
        [forms_shape],
        [],
        edge,
        edge_other,
        couple_near,
        *(x for k in sooner for x in (packs[k], swapped[k])),
    )
    forms, send, send_map, leaving, entering, pi, sigma, response, shift = call(
        functools.partial(solve_kernel, later),
        [V] * (1 + 2 * len(later) + GROUP),
        [forms_shape, ((columns, 2 * surface), BF16), (thin, BF16)]
        + [(joint, F32)] * 2
        + [(thin, F32)] * 2
        + [(joint, F32), (square, F32)],
        [
            ((GROUP, columns, 2 * surface), BF16),
            ((GROUP,) + joint, F32),
            ((GROUP + 1,) + joint, F32),
        ],
        forms,
        *(x for k in later for x in (packs[k], swapped[k])),
        vectors,
        *gathered,
        aliases={0: 0},
    )
    gamma, back_whole = call(
        gamma_kernel, [V], [(square, F32), (square, F32)], [((GROUP + 1,) + square, F32)], forms
    )
    first = send[half:columns]
    bit = GROUP
    if 2 * bit < slabs:
        first = first.astype(F32)
        row = lax.axis_index("row")

        def joined(part):
            other = across(part)
            return jnp.where(
                row == 0, jnp.concatenate([part, other], 0), jnp.concatenate([other, part], 0)
            )

        leave, a_map = leaving[:half], joined(leaving[half:])
        back, d_map = entering[:half], joined(entering[half:])
        alpha, delta = joined(response[:half]), joined(response[half:])
        c_map = back_whole
    while 2 * bit < slabs:
        right = (slab // bit) % 2 == 1

        def sides(own):
            seen = partner(own, bit)
            return jnp.where(right, seen, own), jnp.where(right, own, seen)

        (ax, ay), (cx, cy), (dx, dy) = sides(a_map), sides(c_map), sides(d_map)
        (wx, wy), (fx, fy) = sides(shift), sides(first)
        (px, py), (qx, qy) = sides(leave), sides(back)
        middle = px + compute(wx, fy)
        entry = qy + compute(dy, middle)
        carried = compute(dy, ax)
        pi = pi + jnp.where(right, compute(alpha, middle), 0.0)
        sigma = sigma + jnp.where(right, compute(delta, middle), compute(gamma, entry))
        delta = jnp.where(right, compute(delta, ax), delta + compute(gamma, carried))
        alpha = jnp.where(right, compute(alpha, ax), alpha)
        gamma = jnp.where(right, gamma, compute(gamma, cy))
        leave, back = py + compute(ay, middle), qx + compute(cx, entry)
        a_map, c_map, d_map = compute(ay, ax), compute(cx, cy), dx + compute(cx, carried)
        shift, first = wy, fx
        bit *= 2
        if 2 * bit == slabs:
            left = slab < slabs // 2
            send = jnp.concatenate([jnp.where(left, leave, back), first], axis=0).astype(BF16)
            send_map = lax.dynamic_slice_in_dim(
                jnp.where(left, shift, d_map).astype(BF16),
                row * half,
                half,
                0,
            )
            first = first.astype(BF16)
            leaving = jnp.concatenate([leave, leave], axis=0)
            response = jnp.concatenate(
                [lax.dynamic_slice_in_dim(x, row * half, half, 0) for x in (alpha, delta)], axis=0
            )
    map_seen = partner(send_map, slabs // 2)
    seen = partner(send, slabs // 2)
    response_other = across(response)
    map_other = across(map_seen)
    hand, base = call(
        ready_kernel,
        [V] * 6,
        [((4, 2 * surface, 2 * surface), BF16), (thin, F32)],
        [((2,) + square, F32)],
        couple_near,
        sigma,
        response,
        response_other,
        gamma,
        shift,
    )
    (closed,) = call(
        close_kernel,
        [V] * 8,
        [((columns, 2 * surface), BF16)],
        [((surface, 2 * surface), BF16)],
        hand,
        base,
        pi,
        leaving,
        first,
        seen,
        map_seen,
        map_other,
    )
    (result,) = call(
        final_kernel,
        [V] * 5,
        [((2, shard_rows, columns), F32)],
        [((2, columns, 2 * surface), BF16)],
        count,
        green_blocks,
        direct,
        closed,
        across(closed),
        keep=True,
    )
    return result


def solution(mesh):
    placed = (
        P(None, ("energy", "slab", "row"), None),
        P(None, "slab", None),
        P(None, ("energy", "slab", "row"), None),
        P("slab"),
    )
    return jax.shard_map(
        body,
        mesh=mesh,
        in_specs=placed,
        out_specs=P(None, ("energy", "slab", "row"), None),
        check_vma=False,
    )
```

```python
import functools

import jax
import jax.numpy as jnp
from jax import lax
from jax.experimental import pallas as pl
from jax.experimental.pallas import tpu as pltpu
from jax.sharding import PartitionSpec as P


F32 = jnp.float32
BF16 = jnp.bfloat16
GROUP = 4
ORDER = (3, 2, 1)
EARLY = 2


def contract(x, matrix, across):
    return lax.dot_general(
        x, matrix, (((1,), (1 if across else 0,)), ((), ())), preferred_element_type=F32
    )


def split(x):
    high = x.astype(BF16)
    return high, (x - high.astype(F32)).astype(BF16)


def apply(real_form, x, across=True):
    high, low = split(x)
    both = contract(jnp.concatenate([high, low], axis=0), real_form, across)
    return both[: x.shape[0]] + both[x.shape[0] :]


def apply_short(real_form, x, across=True):
    return contract(x.astype(BF16), real_form, across)


def turned(x):
    half = x.shape[1] // 2
    return jnp.concatenate([-x[:, half:], x[:, :half]], axis=1)


def stacked(x):
    return jnp.concatenate([x, turned(x)], axis=0)


def run_copies(pairs, sems):
    copies = [pltpu.make_async_copy(a, b, sems.at[n]) for n, (a, b) in enumerate(pairs)]
    for c in copies:
        c.start()
    for c in copies:
        c.wait()


def own_rows(green, surface):
    row = lax.axis_index("row")
    return pl.ds(pl.multiple_of(row * (green.shape[1] - surface), surface), surface)


def pack_kernel(green, coupling, pack, sems):
    surface = pack.shape[1]
    rows = own_rows(green, surface)
    last = pl.ds(green.shape[2] - surface, surface)
    part = pl.ds(lax.axis_index("row"), 1)
    run_copies(
        [
            (green.at[:, rows, pl.ds(0, surface)], pack.at[pl.ds(0, 2)]),
            (green.at[:, rows, last], pack.at[pl.ds(2, 2)]),
            (coupling.at[part], pack.at[pl.ds(4, 1)]),
        ],
        sems,
    )


def near_kernel(green, coupling, source, pack, edge, source_near, couple_near, sems):
    rows = own_rows(green, edge.shape[1])
    run_copies(
        [(green.at[:, rows], edge), (source, source_near), (coupling, couple_near)], sems
    )


def masked_source(count, own, other, surface):
    row = lax.axis_index("row")
    orbitals = 2 * own.shape[1]

    def masked(part):
        mine, theirs = own[part].astype(F32), other[part].astype(F32)
        whole = jnp.concatenate(
            [jnp.where(row == 0, mine, theirs), jnp.where(row == 0, theirs, mine)], axis=0
        )
        orbital = lax.broadcasted_iota(jnp.int32, whole.shape, 0)
        live = (orbital < surface + count[:1]) | (orbital >= orbitals - surface)
        return jnp.where(live, whole, 0.0)

    real, imag = masked(0), masked(1)
    return (
        jnp.concatenate([real, imag], axis=1).astype(BF16),
        jnp.concatenate([-imag, real], axis=1).astype(BF16),
    )


def edge_kernel(count, edge, edge_other, source_own, source_other, vectors):
    row = lax.axis_index("row")
    surface = edge.shape[1]
    columns = source_own.shape[2]
    half = columns // 2
    above, below = masked_source(count, source_own, source_other, surface)

    def surface_rows(blocks):
        x = contract(blocks[0], above, False) + contract(blocks[1], below, False)
        whole = jnp.concatenate([x[:, :columns].T, x[:, columns:].T], axis=1)
        return jnp.where(row == 0, whole[:half], whole[half:]).astype(BF16)

    own, other = surface_rows(edge), surface_rows(edge_other)

    @pl.when(row == 0)
    def _():
        vectors[:half] = own
        vectors[half:] = other

    @pl.when(row == 1)
    def _():
        vectors[:half] = other
        vectors[half:] = own


def direct_kernel(count, green, source_own, source_other, surfaces, direct):
    above, below = masked_source(count, source_own, source_other, surfaces.shape[1] // 2)
    direct[...] = contract(green[0], above, False) + contract(green[1], below, False)


def unit_rows(start, count, size):
    eye = (
        start + lax.broadcasted_iota(jnp.int32, (count, size), 0)
        == lax.broadcasted_iota(jnp.int32, (count, size), 1)
    ).astype(F32)
    return jnp.concatenate([eye, jnp.zeros_like(eye)], axis=1)


NEAR, COUPLE, ALONG, BACK, SHIFT = 0, 1, 2, 4, 6


def apply_pair(x, forms, index, name):
    at = (name,) if index is None else (index, name)
    high, low = split(x)
    both = contract(jnp.concatenate([high, low], axis=0), forms[at], False)
    rest = contract(high, forms[at[:-1] + (name + 1,)], False)
    return both[: x.shape[0]] + both[x.shape[0] :] + rest


def columns_of(forms, index, name, rows=None):
    rows = pl.ds(0, forms.shape[2] // 2) if rows is None else rows
    return forms[index, name, rows].astype(F32) + forms[index, name + 1, rows].astype(F32)


def real_form(re, im):
    return jnp.concatenate(
        [jnp.concatenate([re, -im], axis=1), jnp.concatenate([im, re], axis=1)], axis=0
    )


def form_slab(forms, k, near, far_first, far_last, along, b):
    slab = lax.axis_index("slab")
    slabs = lax.axis_size("slab")
    member = slab % GROUP
    known = slab - member + (member ^ k) < slabs - 1
    b_re, b_im = (jnp.where(known, x, jnp.zeros_like(x)) for x in b)
    couple = real_form(b_re, b_im)
    forms[k, NEAR] = real_form(*near)
    forms[k, COUPLE] = couple

    def transposed(re, im):
        return jnp.concatenate([re.astype(F32).T, im.astype(F32).T], axis=1).astype(BF16)

    def keep(name, x):
        high, low = split(stacked(x))
        forms[k, name] = high
        forms[k, name + 1] = low

    b_columns = transposed(b_re, b_im)
    keep(ALONG, contract(transposed(*along), couple, False))
    keep(BACK, contract(b_columns, real_form(*far_first), True))
    keep(SHIFT, apply(couple, contract(b_columns, real_form(*far_last), True), False))


def form_kernel(order, *refs):
    edge, edge_other, coupling = refs[:3]
    packs, forms = refs[3:-1], refs[-1]
    row = lax.axis_index("row")
    size = coupling.shape[1]
    width = edge.shape[2]

    def fill(first_is_own):
        f, l = (edge, edge_other) if first_is_own else (edge_other, edge)

        def corner(ref, start):
            return ref[0, :, start : start + size], ref[1, :, start : start + size]

        last = width - size
        form_slab(
            forms,
            0,
            corner(f, 0),
            corner(f, last),
            corner(l, last),
            corner(l, 0),
            (coupling[0], coupling[1]),
        )
        for n, k in enumerate(order):
            form_packed(forms, k, packs[2 * n], packs[2 * n + 1], first_is_own)

    @pl.when(row == 0)
    def _():
        fill(True)

    @pl.when(row == 1)
    def _():
        fill(False)


def form_packed(forms, k, mine, other, first_is_own):
    f, l = (mine, other) if first_is_own else (other, mine)
    form_slab(forms, k, (f[0], f[1]), (f[2], f[3]), (l[2], l[3]), (l[0], l[1]), (f[4], l[4]))


def solve_kernel(
    later, _, *refs
):
    packed, given = refs[: 2 * len(later)], refs[2 * len(later) : 2 * len(later) + GROUP]
    forms, send, send_map, leaving, entering, pi, sigma, response, shift, vectors, states, backs = refs[
        2 * len(later) + GROUP :
    ]
    row = lax.axis_index("row")
    slab = lax.axis_index("slab")
    slabs = lax.axis_size("slab")
    member = slab % GROUP
    size = shift.shape[0]
    half = vectors.shape[1] // 2

    def fill(first_is_own):
        for n, k in enumerate(later):
            form_packed(forms, k, packed[2 * n], packed[2 * n + 1], first_is_own)

    @pl.when(row == 0)
    def _():
        fill(True)

    @pl.when(row == 1)
    def _():
        fill(False)

    for k, v in enumerate(given):
        vectors[member ^ k] = v[...]
    first = [vectors[i, :half] for i in range(GROUP)]
    rows = pl.ds(pl.multiple_of(row * half, half), half)
    unit = unit_rows(row * half, half, size)
    nothing = jnp.zeros_like(unit)

    def beside(x, below=nothing):
        return jnp.concatenate([x, below], axis=0)

    terms = []
    for i in range(GROUP):
        term = contract(vectors[i, half:], forms[member ^ i, COUPLE], False)
        if i < GROUP - 1:
            term = term + contract(first[i + 1], forms[member ^ i, SHIFT], False)
            term = term + contract(first[i + 1], forms[member ^ i, SHIFT + 1], False)
        terms.append(term)
    states[0] = beside(jnp.zeros_like(terms[0]), unit)
    u = beside(terms[0], columns_of(forms, member, ALONG, rows))
    for i in range(1, GROUP - 1):
        states[i] = u
        u = apply_pair(u, forms, member ^ i, ALONG) + beside(terms[i])
    states[GROUP - 1] = u
    last = member ^ (GROUP - 1)
    s = apply(forms[last, NEAR], u) + beside(first[GROUP - 1].astype(F32))
    if 2 * GROUP < slabs:
        u = apply_pair(u, forms, last, ALONG) + beside(terms[GROUP - 1])
        leaving[...] = u
    else:
        u = apply_pair(u[:half], forms, last, ALONG) + terms[GROUP - 1]
        leaving[:half] = u
        leaving[half:] = nothing
    backs[GROUP] = jnp.zeros_like(s)
    backs[GROUP - 1] = s
    for i in reversed(range(GROUP - 1)):
        near = forms[member ^ i, NEAR]
        if i:
            e = apply(near, states[i]) + beside(first[i].astype(F32))
        else:
            e = beside(first[i].astype(F32), apply_short(near, unit))
        s = e + apply_pair(s, forms, member ^ i, BACK)
        backs[i] = s
    entering[...] = s
    shift[...] = columns_of(forms, last, SHIFT)
    left = slab < slabs // 2
    send[:half] = jnp.where(left, u[:half], s[:half]).astype(BF16)
    send[half:] = first[0]
    send_map[...] = jnp.where(left, columns_of(forms, last, SHIFT, rows), s[half:]).astype(BF16)
    here, after = states[member], backs[member + 1]
    pi[...] = here[:half]
    sigma[...] = after[:half]
    response[:half] = here[half:]
    response[half:] = after[half:]


def gamma_kernel(forms, gamma, whole, backs):
    member = lax.axis_index("slab") % GROUP
    backs[GROUP] = unit_rows(0, gamma.shape[0], gamma.shape[0])
    s = columns_of(forms, member ^ (GROUP - 1), BACK)
    backs[GROUP - 1] = s
    for i in reversed(range(GROUP - 1)):
        s = apply_pair(s, forms, member ^ i, BACK)
        backs[i] = s
    whole[...] = s
    gamma[...] = backs[member + 1]


def ready_kernel(coupling, sigma, response, response_other, gamma, shift, hand, base, whole):
    row = lax.axis_index("row")
    half = base.shape[0]
    left = lax.axis_index("slab") < lax.axis_size("slab") // 2
    b = real_form(coupling[0], coupling[1])

    def place(first, second):
        for i in range(2):
            whole[i, :half] = first[i * half : (i + 1) * half]
            whole[i, half:] = second[i * half : (i + 1) * half]

    @pl.when(row == 0)
    def _():
        place(response, response_other)

    @pl.when(row == 1)
    def _():
        place(response_other, response)

    def keep(index, x):
        hand[index], hand[index + 1] = split(stacked(x))

    keep(0, jnp.where(left, shift[...], whole[0]))
    keep(2, apply(b, jnp.where(left, gamma[...], whole[1])))
    base[...] = apply(b, sigma[...])


def merge_kernel(hand, base, pi, leaving, first, map_seen, map_other, ends, ahead_map, rows):
    row = lax.axis_index("row")
    half = first.shape[0]
    part = map_seen.shape[0]
    left = lax.axis_index("slab") < lax.axis_size("slab") // 2

    @pl.when(row == 0)
    def _():
        rows[:part] = map_seen[...]
        rows[part:] = map_other[...]

    @pl.when(row == 1)
    def _():
        rows[:part] = map_other[...]
        rows[part:] = map_seen[...]

    map_form = stacked(rows[...])
    ends[0] = pi[...]

    @pl.when(left)
    def _():
        size = rows.shape[0]
        w = hand[0, :size].astype(F32) + hand[1, :size].astype(F32)
        both = jnp.concatenate([leaving[:half], w], axis=0)
        both = apply_pair(apply(map_form, both, False), hand, None, 2)
        ends[1] = base[...] + both[:half]
        ahead_map[0], ahead_map[1] = split(stacked(both[half:]))

    @pl.when(jnp.logical_not(left))
    def _():
        w = apply_short(map_form, first[...], False)
        ends[0] = pi[...] + apply_pair(w, hand, None, 0)
        ends[1] = base[...] + apply_pair(w, hand, None, 2)


def close_kernel(hand, ends, ahead_map, seen, out):
    half = ends.shape[1]
    left = lax.axis_index("slab") < lax.axis_size("slab") // 2
    there = seen[:half]
    upper = ends[1] + contract(there, hand[2], False) + contract(there, hand[3], False)

    @pl.when(left)
    def _():
        ahead = seen[half:]
        more = contract(ahead, ahead_map[0], False) + contract(ahead, ahead_map[1], False)
        out[:half] = ends[0].astype(BF16)
        out[half:] = (upper + more).astype(BF16)

    @pl.when(jnp.logical_not(left))
    def _():
        more = contract(there, hand[0], False) + contract(there, hand[1], False)
        out[:half] = (ends[0] + more).astype(BF16)
        out[half:] = upper.astype(BF16)


def final_kernel(count, green, direct, own, other, result, whole):
    row = lax.axis_index("row")
    shard_rows, width = green.shape[1:]
    half = own.shape[0] // 2
    columns = 2 * half
    surface = own.shape[1] // 2

    def place(first, second):
        for i in range(2):
            whole[i, :half] = first[i * half : (i + 1) * half]
            whole[i, half:] = second[i * half : (i + 1) * half]

    @pl.when(row == 0)
    def _():
        place(own, other)

    @pl.when(row == 1)
    def _():
        place(other, own)

    total = direct[...]
    for start, x in ((0, whole[0]), (width - surface, whole[1])):
        cols = slice(start, start + surface)
        g = jnp.concatenate([green[0, :, cols], green[1, :, cols]], axis=1)
        total = total + contract(g, real_form(x[:, :surface], x[:, surface:]), True)
    orbital = row * shard_rows + lax.broadcasted_iota(jnp.int32, total.shape, 0)
    limit = jnp.concatenate([count[:1]] * (total.shape[1] // count.shape[1]), axis=1)
    live = (orbital < surface + limit) | (orbital >= width - surface)
    total = jnp.where(live, total, 0.0)
    result[0] = total[:, :columns]
    result[1] = total[:, columns:]


V, H = (pl.BlockSpec(memory_space=m) for m in (pltpu.VMEM, pltpu.HBM))


def call(kernel, specs, outs, scratch, *args, keep=False, aliases={}):
    args = [
        pltpu.with_memory_space_constraint(a, s.memory_space)
        for a, s in zip(args, specs, strict=True)
    ]
    kind = jax.ShapeDtypeStruct if keep else pltpu.VMEM
    return pl.pallas_call(
        kernel,
        in_specs=specs,
        out_specs=[V] * len(outs),
        out_shape=[kind(s, d) for s, d in outs],
        scratch_shapes=[pltpu.VMEM(*x) if isinstance(x, tuple) else x for x in scratch],
        input_output_aliases=aliases,
        compiler_params=pltpu.CompilerParams(vmem_limit_bytes=24 << 20),
    )(*args)


def compute(columns, x):
    size = columns.shape[1] // 2

    def mul(a, b):
        return jnp.dot(a, b, preferred_element_type=F32, precision=lax.Precision.HIGHEST)

    c_re, c_im = columns[:, :size], columns[:, size:]
    x_re, x_im = x[:, :size], x[:, size:]
    return jnp.concatenate([mul(x_re, c_re) - mul(x_im, c_im), mul(x_re, c_im) + mul(x_im, c_re)], axis=1)


def body(green_blocks, coupling, source, interior_count):
    shard_rows = green_blocks.shape[1]
    width = green_blocks.shape[2]
    surface = coupling.shape[1]
    columns = source.shape[2]
    half = columns // 2
    slab = lax.axis_index("slab")
    slabs = lax.axis_size("slab")

    def across(x):
        return lax.ppermute(x, "row", [(0, 1), (1, 0)])

    def partner(x, bit):
        return lax.ppermute(x, "slab", [(i, i ^ bit) for i in range(slabs)])

    square = (surface, 2 * surface)
    thin, joint = (half, 2 * surface), (columns, 2 * surface)
    (pack,) = call(
        pack_kernel,
        [H] * 2,
        [((5, surface, surface), BF16)],
        [pltpu.SemaphoreType.DMA((3,))],
        green_blocks,
        coupling,
    )
    edge, source_near, couple_near = call(
        near_kernel,
        [H] * 3 + [V],
        [((2, surface, width), BF16), (source.shape, BF16), (coupling.shape, BF16)],
        [pltpu.SemaphoreType.DMA((3,))],
        green_blocks,
        coupling,
        source,
        pack,
    )
    count = jnp.broadcast_to(interior_count.reshape(1, 1), (8, columns))
    source_other = across(source)
    edge_other = across(edge)
    packs = {}
    for k in ORDER:
        packs[k] = partner(pack, k)
    (vectors,) = call(
        edge_kernel,
        [V] * 5,
        [((columns, 2 * surface), BF16)],
        [],
        count,
        edge,
        edge_other,
        source_near,
        source_other,
    )
    (direct,) = call(
        direct_kernel,
        [V] * 5,
        [((shard_rows, 2 * columns), F32)],
        [],
        count,
        green_blocks,
        source_near,
        source_other,
        vectors,
    )
    gathered = []
    for k in range(1, GROUP):
        gathered.append(partner(vectors, k))
    swapped = {}
    for k in ORDER:
        swapped[k] = across(packs[k])
    sooner, later = ORDER[:EARLY], ORDER[EARLY:]
    forms_shape = ((GROUP, 8, 2 * surface, 2 * surface), BF16)
    (forms,) = call(
        functools.partial(form_kernel, sooner),
        [V] * (3 + 2 * len(sooner)),
        [forms_shape],
        [],
        edge,
        edge_other,
        couple_near,
        *(x for k in sooner for x in (packs[k], swapped[k])),
    )
    forms, send, send_map, leaving, entering, pi, sigma, response, shift = call(
        functools.partial(solve_kernel, later),
        [V] * (1 + 2 * len(later) + GROUP),
        [forms_shape, ((columns, 2 * surface), BF16), (thin, BF16)]
        + [(joint, F32)] * 2
        + [(thin, F32)] * 2
        + [(joint, F32), (square, F32)],
        [
            ((GROUP, columns, 2 * surface), BF16),
            ((GROUP,) + joint, F32),
            ((GROUP + 1,) + joint, F32),
        ],
        forms,
        *(x for k in later for x in (packs[k], swapped[k])),
        vectors,
        *gathered,
        aliases={0: 0},
    )
    gamma, back_whole = call(
        gamma_kernel, [V], [(square, F32), (square, F32)], [((GROUP + 1,) + square, F32)], forms
    )
    first = send[half:columns]
    bit = GROUP
    if 2 * bit < slabs:
        first = first.astype(F32)
        row = lax.axis_index("row")

        def joined(part):
            other = across(part)
            return jnp.where(
                row == 0, jnp.concatenate([part, other], 0), jnp.concatenate([other, part], 0)
            )

        leave, a_map = leaving[:half], joined(leaving[half:])
        back, d_map = entering[:half], joined(entering[half:])
        alpha, delta = joined(response[:half]), joined(response[half:])
        c_map = back_whole
    while 2 * bit < slabs:
        right = (slab // bit) % 2 == 1

        def sides(own):
            seen = partner(own, bit)
            return jnp.where(right, seen, own), jnp.where(right, own, seen)

        (ax, ay), (cx, cy), (dx, dy) = sides(a_map), sides(c_map), sides(d_map)
        (wx, wy), (fx, fy) = sides(shift), sides(first)
        (px, py), (qx, qy) = sides(leave), sides(back)
        middle = px + compute(wx, fy)
        entry = qy + compute(dy, middle)
        carried = compute(dy, ax)
        pi = pi + jnp.where(right, compute(alpha, middle), 0.0)
        sigma = sigma + jnp.where(right, compute(delta, middle), compute(gamma, entry))
        delta = jnp.where(right, compute(delta, ax), delta + compute(gamma, carried))
        alpha = jnp.where(right, compute(alpha, ax), alpha)
        gamma = jnp.where(right, gamma, compute(gamma, cy))
        leave, back = py + compute(ay, middle), qx + compute(cx, entry)
        a_map, c_map, d_map = compute(ay, ax), compute(cx, cy), dx + compute(cx, carried)
        shift, first = wy, fx
        bit *= 2
        if 2 * bit == slabs:
            left = slab < slabs // 2
            send = jnp.concatenate([jnp.where(left, leave, back), first], axis=0).astype(BF16)
            send_map = lax.dynamic_slice_in_dim(
                jnp.where(left, shift, d_map).astype(BF16),
                row * half,
                half,
                0,
            )
            first = first.astype(BF16)
            leaving = jnp.concatenate([leave, leave], axis=0)
            response = jnp.concatenate(
                [lax.dynamic_slice_in_dim(x, row * half, half, 0) for x in (alpha, delta)], axis=0
            )
    map_seen = partner(send_map, slabs // 2)
    seen = partner(send, slabs // 2)
    response_other = across(response)
    map_other = across(map_seen)
    hand, base = call(
        ready_kernel,
        [V] * 6,
        [((4, 2 * surface, 2 * surface), BF16), (thin, F32)],
        [((2,) + square, F32)],
        couple_near,
        sigma,
        response,
        response_other,
        gamma,
        shift,
    )
    ends, ahead_map = call(
        merge_kernel,
        [V] * 7,
        [((2,) + thin, F32), ((2, 2 * surface, 2 * surface), BF16)],
        [(square, BF16)],
        hand,
        base,
        pi,
        leaving,
        first,
        map_seen,
        map_other,
    )
    (closed,) = call(
        close_kernel, [V] * 4, [((columns, 2 * surface), BF16)], [], hand, ends, ahead_map, seen
    )
    (result,) = call(
        final_kernel,
        [V] * 5,
        [((2, shard_rows, columns), F32)],
        [((2, columns, 2 * surface), BF16)],
        count,
        green_blocks,
        direct,
        closed,
        across(closed),
        keep=True,
    )
    return result


def solution(mesh):
    placed = (
        P(None, ("energy", "slab", "row"), None),
        P(None, "slab", None),
        P(None, ("energy", "slab", "row"), None),
        P("slab"),
    )
    return jax.shard_map(
        body,
        mesh=mesh,
        in_specs=placed,
        out_specs=P(None, ("energy", "slab", "row"), None),
        check_vma=False,
    )
```

```python
import functools

import jax
import jax.numpy as jnp
from jax import lax
from jax.experimental import pallas as pl
from jax.experimental.pallas import tpu as pltpu
from jax.sharding import PartitionSpec as P


F32 = jnp.float32
BF16 = jnp.bfloat16
GROUP = 4
ORDER = (3, 2, 1)
EARLY = 2


def contract(x, matrix, across):
    return lax.dot_general(
        x, matrix, (((1,), (1 if across else 0,)), ((), ())), preferred_element_type=F32
    )


def split(x):
    high = x.astype(BF16)
    return high, (x - high.astype(F32)).astype(BF16)


def apply(real_form, x, across=True):
    high, low = split(x)
    both = contract(jnp.concatenate([high, low], axis=0), real_form, across)
    return both[: x.shape[0]] + both[x.shape[0] :]


def apply_short(real_form, x, across=True):
    return contract(x.astype(BF16), real_form, across)


def turned(x):
    half = x.shape[1] // 2
    return jnp.concatenate([-x[:, half:], x[:, :half]], axis=1)


def stacked(x):
    return jnp.concatenate([x, turned(x)], axis=0)


def run_copies(pairs, sems):
    copies = [pltpu.make_async_copy(a, b, sems.at[n]) for n, (a, b) in enumerate(pairs)]
    for c in copies:
        c.start()
    for c in copies:
        c.wait()


def own_rows(green, surface):
    row = lax.axis_index("row")
    return pl.ds(pl.multiple_of(row * (green.shape[1] - surface), surface), surface)


def pack_kernel(green, coupling, pack, sems):
    surface = pack.shape[1]
    rows = own_rows(green, surface)
    last = pl.ds(green.shape[2] - surface, surface)
    part = pl.ds(lax.axis_index("row"), 1)
    run_copies(
        [
            (green.at[:, rows, pl.ds(0, surface)], pack.at[pl.ds(0, 2)]),
            (green.at[:, rows, last], pack.at[pl.ds(2, 2)]),
            (coupling.at[part], pack.at[pl.ds(4, 1)]),
        ],
        sems,
    )


def near_kernel(green, coupling, source, pack, edge, source_near, couple_near, sems):
    rows = own_rows(green, edge.shape[1])
    run_copies(
        [(green.at[:, rows], edge), (source, source_near), (coupling, couple_near)], sems
    )


def masked_source(count, own, other, surface):
    row = lax.axis_index("row")
    orbitals = 2 * own.shape[1]

    def masked(part):
        mine, theirs = own[part].astype(F32), other[part].astype(F32)
        whole = jnp.concatenate(
            [jnp.where(row == 0, mine, theirs), jnp.where(row == 0, theirs, mine)], axis=0
        )
        orbital = lax.broadcasted_iota(jnp.int32, whole.shape, 0)
        live = (orbital < surface + count[:1]) | (orbital >= orbitals - surface)
        return jnp.where(live, whole, 0.0)

    real, imag = masked(0), masked(1)
    return (
        jnp.concatenate([real, imag], axis=1).astype(BF16),
        jnp.concatenate([-imag, real], axis=1).astype(BF16),
    )


def edge_kernel(count, edge, edge_other, source_own, source_other, vectors):
    row = lax.axis_index("row")
    surface = edge.shape[1]
    columns = source_own.shape[2]
    half = columns // 2
    above, below = masked_source(count, source_own, source_other, surface)

    def surface_rows(blocks):
        x = contract(blocks[0], above, False) + contract(blocks[1], below, False)
        whole = jnp.concatenate([x[:, :columns].T, x[:, columns:].T], axis=1)
        return jnp.where(row == 0, whole[:half], whole[half:]).astype(BF16)

    own, other = surface_rows(edge), surface_rows(edge_other)

    @pl.when(row == 0)
    def _():
        vectors[:half] = own
        vectors[half:] = other

    @pl.when(row == 1)
    def _():
        vectors[:half] = other
        vectors[half:] = own


def direct_kernel(count, green, source_own, source_other, surfaces, direct):
    above, below = masked_source(count, source_own, source_other, surfaces.shape[1] // 2)
    direct[...] = contract(green[0], above, False) + contract(green[1], below, False)


def unit_rows(start, count, size):
    eye = (
        start + lax.broadcasted_iota(jnp.int32, (count, size), 0)
        == lax.broadcasted_iota(jnp.int32, (count, size), 1)
    ).astype(F32)
    return jnp.concatenate([eye, jnp.zeros_like(eye)], axis=1)


NEAR, COUPLE, ALONG, BACK, SHIFT = 0, 1, 2, 4, 6


def apply_pair(x, forms, index, name):
    at = (name,) if index is None else (index, name)
    high, low = split(x)
    both = contract(jnp.concatenate([high, low], axis=0), forms[at], False)
    rest = contract(high, forms[at[:-1] + (name + 1,)], False)
    return both[: x.shape[0]] + both[x.shape[0] :] + rest


def columns_of(forms, index, name, rows=None):
    rows = pl.ds(0, forms.shape[2] // 2) if rows is None else rows
    return forms[index, name, rows].astype(F32) + forms[index, name + 1, rows].astype(F32)


def real_form(re, im):
    return jnp.concatenate(
        [jnp.concatenate([re, -im], axis=1), jnp.concatenate([im, re], axis=1)], axis=0
    )


def form_slab(forms, k, near, far_first, far_last, along, b):
    slab = lax.axis_index("slab")
    slabs = lax.axis_size("slab")
    member = slab % GROUP
    known = slab - member + (member ^ k) < slabs - 1
    b_re, b_im = (jnp.where(known, x, jnp.zeros_like(x)) for x in b)
    couple = real_form(b_re, b_im)
    forms[k, NEAR] = real_form(*near)
    forms[k, COUPLE] = couple

    def transposed(re, im):
        return jnp.concatenate([re.astype(F32).T, im.astype(F32).T], axis=1).astype(BF16)

    def keep(name, x):
        high, low = split(stacked(x))
        forms[k, name] = high
        forms[k, name + 1] = low

    b_columns = transposed(b_re, b_im)
    keep(ALONG, contract(transposed(*along), couple, False))
    keep(BACK, contract(b_columns, real_form(*far_first), True))
    keep(SHIFT, apply(couple, contract(b_columns, real_form(*far_last), True), False))


def form_kernel(order, *refs):
    edge, edge_other, coupling = refs[:3]
    packs, forms = refs[3:-1], refs[-1]
    row = lax.axis_index("row")
    size = coupling.shape[1]
    width = edge.shape[2]

    def fill(first_is_own):
        f, l = (edge, edge_other) if first_is_own else (edge_other, edge)

        def corner(ref, start):
            return ref[0, :, start : start + size], ref[1, :, start : start + size]

        last = width - size
        form_slab(
            forms,
            0,
            corner(f, 0),
            corner(f, last),
            corner(l, last),
            corner(l, 0),
            (coupling[0], coupling[1]),
        )
        for n, k in enumerate(order):
            form_packed(forms, k, packs[2 * n], packs[2 * n + 1], first_is_own)

    @pl.when(row == 0)
    def _():
        fill(True)

    @pl.when(row == 1)
    def _():
        fill(False)


def form_packed(forms, k, mine, other, first_is_own):
    f, l = (mine, other) if first_is_own else (other, mine)
    form_slab(forms, k, (f[0], f[1]), (f[2], f[3]), (l[2], l[3]), (l[0], l[1]), (f[4], l[4]))


def more_kernel(later, _, *refs):
    packed, forms = refs[:-1], refs[-1]
    row = lax.axis_index("row")

    def fill(first_is_own):
        for n, k in enumerate(later):
            form_packed(forms, k, packed[2 * n], packed[2 * n + 1], first_is_own)

    @pl.when(row == 0)
    def _():
        fill(True)

    @pl.when(row == 1)
    def _():
        fill(False)


def solve_kernel(forms, *refs):
    given = refs[:GROUP]
    send, send_map, leaving, entering, pi, sigma, response, shift, vectors, states, backs = refs[
        GROUP:
    ]
    row = lax.axis_index("row")
    slab = lax.axis_index("slab")
    slabs = lax.axis_size("slab")
    member = slab % GROUP
    size = shift.shape[0]
    half = vectors.shape[1] // 2

    for k, v in enumerate(given):
        vectors[member ^ k] = v[...]
    first = [vectors[i, :half] for i in range(GROUP)]
    rows = pl.ds(pl.multiple_of(row * half, half), half)
    unit = unit_rows(row * half, half, size)
    nothing = jnp.zeros_like(unit)

    def beside(x, below=nothing):
        return jnp.concatenate([x, below], axis=0)

    terms = []
    for i in range(GROUP):
        term = contract(vectors[i, half:], forms[member ^ i, COUPLE], False)
        if i < GROUP - 1:
            term = term + contract(first[i + 1], forms[member ^ i, SHIFT], False)
            term = term + contract(first[i + 1], forms[member ^ i, SHIFT + 1], False)
        terms.append(term)
    states[0] = beside(jnp.zeros_like(terms[0]), unit)
    u = beside(terms[0], columns_of(forms, member, ALONG, rows))
    for i in range(1, GROUP - 1):
        states[i] = u
        u = apply_pair(u, forms, member ^ i, ALONG) + beside(terms[i])
    states[GROUP - 1] = u
    last = member ^ (GROUP - 1)
    s = apply(forms[last, NEAR], u) + beside(first[GROUP - 1].astype(F32))
    if 2 * GROUP < slabs:
        u = apply_pair(u, forms, last, ALONG) + beside(terms[GROUP - 1])
        leaving[...] = u
    else:
        u = apply_pair(u[:half], forms, last, ALONG) + terms[GROUP - 1]
        leaving[:half] = u
        leaving[half:] = nothing
    backs[GROUP] = jnp.zeros_like(s)
    backs[GROUP - 1] = s
    for i in reversed(range(GROUP - 1)):
        near = forms[member ^ i, NEAR]
        if i:
            e = apply(near, states[i]) + beside(first[i].astype(F32))
        else:
            e = beside(first[i].astype(F32), apply_short(near, unit))
        s = e + apply_pair(s, forms, member ^ i, BACK)
        backs[i] = s
    entering[...] = s
    shift[...] = columns_of(forms, last, SHIFT)
    left = slab < slabs // 2
    send[:half] = jnp.where(left, u[:half], s[:half]).astype(BF16)
    send[half:] = first[0]
    send_map[...] = jnp.where(left, columns_of(forms, last, SHIFT, rows), s[half:]).astype(BF16)
    here, after = states[member], backs[member + 1]
    pi[...] = here[:half]
    sigma[...] = after[:half]
    response[:half] = here[half:]
    response[half:] = after[half:]


def gamma_kernel(forms, gamma, whole, backs):
    member = lax.axis_index("slab") % GROUP
    backs[GROUP] = unit_rows(0, gamma.shape[0], gamma.shape[0])
    s = columns_of(forms, member ^ (GROUP - 1), BACK)
    backs[GROUP - 1] = s
    for i in reversed(range(GROUP - 1)):
        s = apply_pair(s, forms, member ^ i, BACK)
        backs[i] = s
    whole[...] = s
    gamma[...] = backs[member + 1]


def ready_kernel(coupling, sigma, response, response_other, gamma, shift, hand, base, whole):
    row = lax.axis_index("row")
    half = base.shape[0]
    left = lax.axis_index("slab") < lax.axis_size("slab") // 2
    b = real_form(coupling[0], coupling[1])

    def place(first, second):
        for i in range(2):
            whole[i, :half] = first[i * half : (i + 1) * half]
            whole[i, half:] = second[i * half : (i + 1) * half]

    @pl.when(row == 0)
    def _():
        place(response, response_other)

    @pl.when(row == 1)
    def _():
        place(response_other, response)

    def keep(index, x):
        hand[index], hand[index + 1] = split(stacked(x))

    keep(0, jnp.where(left, shift[...], whole[0]))
    keep(2, apply(b, jnp.where(left, gamma[...], whole[1])))
    base[...] = apply(b, sigma[...])


def merge_kernel(hand, base, pi, leaving, first, map_seen, map_other, ends, ahead_map, rows):
    row = lax.axis_index("row")
    half = first.shape[0]
    part = map_seen.shape[0]
    left = lax.axis_index("slab") < lax.axis_size("slab") // 2

    @pl.when(row == 0)
    def _():
        rows[:part] = map_seen[...]
        rows[part:] = map_other[...]

    @pl.when(row == 1)
    def _():
        rows[:part] = map_other[...]
        rows[part:] = map_seen[...]

    map_form = stacked(rows[...])
    ends[0] = pi[...]

    @pl.when(left)
    def _():
        size = rows.shape[0]
        w = hand[0, :size].astype(F32) + hand[1, :size].astype(F32)
        both = jnp.concatenate([leaving[:half], w], axis=0)
        both = apply_pair(apply(map_form, both, False), hand, None, 2)
        ends[1] = base[...] + both[:half]
        ahead_map[0], ahead_map[1] = split(stacked(both[half:]))

    @pl.when(jnp.logical_not(left))
    def _():
        w = apply_short(map_form, first[...], False)
        ends[0] = pi[...] + apply_pair(w, hand, None, 0)
        ends[1] = base[...] + apply_pair(w, hand, None, 2)


def close_kernel(hand, ends, ahead_map, seen, out):
    half = ends.shape[1]
    left = lax.axis_index("slab") < lax.axis_size("slab") // 2
    there = seen[:half]
    upper = ends[1] + contract(there, hand[2], False) + contract(there, hand[3], False)

    @pl.when(left)
    def _():
        ahead = seen[half:]
        more = contract(ahead, ahead_map[0], False) + contract(ahead, ahead_map[1], False)
        out[:half] = ends[0].astype(BF16)
        out[half:] = (upper + more).astype(BF16)

    @pl.when(jnp.logical_not(left))
    def _():
        more = contract(there, hand[0], False) + contract(there, hand[1], False)
        out[:half] = (ends[0] + more).astype(BF16)
        out[half:] = upper.astype(BF16)


def final_kernel(count, green, direct, own, other, result, whole):
    row = lax.axis_index("row")
    shard_rows, width = green.shape[1:]
    half = own.shape[0] // 2
    columns = 2 * half
    surface = own.shape[1] // 2

    def place(first, second):
        for i in range(2):
            whole[i, :half] = first[i * half : (i + 1) * half]
            whole[i, half:] = second[i * half : (i + 1) * half]

    @pl.when(row == 0)
    def _():
        place(own, other)

    @pl.when(row == 1)
    def _():
        place(other, own)

    total = direct[...]
    for start, x in ((0, whole[0]), (width - surface, whole[1])):
        cols = slice(start, start + surface)
        g = jnp.concatenate([green[0, :, cols], green[1, :, cols]], axis=1)
        total = total + contract(g, real_form(x[:, :surface], x[:, surface:]), True)
    orbital = row * shard_rows + lax.broadcasted_iota(jnp.int32, total.shape, 0)
    limit = jnp.concatenate([count[:1]] * (total.shape[1] // count.shape[1]), axis=1)
    live = (orbital < surface + limit) | (orbital >= width - surface)
    total = jnp.where(live, total, 0.0)
    result[0] = total[:, :columns]
    result[1] = total[:, columns:]


V, H = (pl.BlockSpec(memory_space=m) for m in (pltpu.VMEM, pltpu.HBM))


def call(kernel, specs, outs, scratch, *args, keep=False, aliases={}):
    args = [
        pltpu.with_memory_space_constraint(a, s.memory_space)
        for a, s in zip(args, specs, strict=True)
    ]
    kind = jax.ShapeDtypeStruct if keep else pltpu.VMEM
    return pl.pallas_call(
        kernel,
        in_specs=specs,
        out_specs=[V] * len(outs),
        out_shape=[kind(s, d) for s, d in outs],
        scratch_shapes=[pltpu.VMEM(*x) if isinstance(x, tuple) else x for x in scratch],
        input_output_aliases=aliases,
        compiler_params=pltpu.CompilerParams(vmem_limit_bytes=24 << 20),
    )(*args)


def compute(columns, x):
    size = columns.shape[1] // 2

    def mul(a, b):
        return jnp.dot(a, b, preferred_element_type=F32, precision=lax.Precision.HIGHEST)

    c_re, c_im = columns[:, :size], columns[:, size:]
    x_re, x_im = x[:, :size], x[:, size:]
    return jnp.concatenate([mul(x_re, c_re) - mul(x_im, c_im), mul(x_re, c_im) + mul(x_im, c_re)], axis=1)


def body(green_blocks, coupling, source, interior_count):
    shard_rows = green_blocks.shape[1]
    width = green_blocks.shape[2]
    surface = coupling.shape[1]
    columns = source.shape[2]
    half = columns // 2
    slab = lax.axis_index("slab")
    slabs = lax.axis_size("slab")

    def across(x):
        return lax.ppermute(x, "row", [(0, 1), (1, 0)])

    def partner(x, bit):
        return lax.ppermute(x, "slab", [(i, i ^ bit) for i in range(slabs)])

    square = (surface, 2 * surface)
    thin, joint = (half, 2 * surface), (columns, 2 * surface)
    (pack,) = call(
        pack_kernel,
        [H] * 2,
        [((5, surface, surface), BF16)],
        [pltpu.SemaphoreType.DMA((3,))],
        green_blocks,
        coupling,
    )
    edge, source_near, couple_near = call(
        near_kernel,
        [H] * 3 + [V],
        [((2, surface, width), BF16), (source.shape, BF16), (coupling.shape, BF16)],
        [pltpu.SemaphoreType.DMA((3,))],
        green_blocks,
        coupling,
        source,
        pack,
    )
    count = jnp.broadcast_to(interior_count.reshape(1, 1), (8, columns))
    source_other = across(source)
    edge_other = across(edge)
    packs = {}
    for k in ORDER:
        packs[k] = partner(pack, k)
    (vectors,) = call(
        edge_kernel,
        [V] * 5,
        [((columns, 2 * surface), BF16)],
        [],
        count,
        edge,
        edge_other,
        source_near,
        source_other,
    )
    (direct,) = call(
        direct_kernel,
        [V] * 5,
        [((shard_rows, 2 * columns), F32)],
        [],
        count,
        green_blocks,
        source_near,
        source_other,
        vectors,
    )
    gathered = []
    for k in range(1, GROUP):
        gathered.append(partner(vectors, k))
    swapped = {}
    for k in ORDER:
        swapped[k] = across(packs[k])
    sooner, later = ORDER[:EARLY], ORDER[EARLY:]
    forms_shape = ((GROUP, 8, 2 * surface, 2 * surface), BF16)
    (forms,) = call(
        functools.partial(form_kernel, sooner),
        [V] * (3 + 2 * len(sooner)),
        [forms_shape],
        [],
        edge,
        edge_other,
        couple_near,
        *(x for k in sooner for x in (packs[k], swapped[k])),
    )
    (forms,) = call(
        functools.partial(more_kernel, later),
        [V] * (1 + 2 * len(later)),
        [forms_shape],
        [],
        forms,
        *(x for k in later for x in (packs[k], swapped[k])),
        aliases={0: 0},
    )
    send, send_map, leaving, entering, pi, sigma, response, shift = call(
        solve_kernel,
        [V] * (1 + GROUP),
        [((columns, 2 * surface), BF16), (thin, BF16)]
        + [(joint, F32)] * 2
        + [(thin, F32)] * 2
        + [(joint, F32), (square, F32)],
        [
            ((GROUP, columns, 2 * surface), BF16),
            ((GROUP,) + joint, F32),
            ((GROUP + 1,) + joint, F32),
        ],
        forms,
        vectors,
        *gathered,
    )
    gamma, back_whole = call(
        gamma_kernel, [V], [(square, F32), (square, F32)], [((GROUP + 1,) + square, F32)], forms
    )
    first = send[half:columns]
    bit = GROUP
    if 2 * bit < slabs:
        first = first.astype(F32)
        row = lax.axis_index("row")

        def joined(part):
            other = across(part)
            return jnp.where(
                row == 0, jnp.concatenate([part, other], 0), jnp.concatenate([other, part], 0)
            )

        leave, a_map = leaving[:half], joined(leaving[half:])
        back, d_map = entering[:half], joined(entering[half:])
        alpha, delta = joined(response[:half]), joined(response[half:])
        c_map = back_whole
    while 2 * bit < slabs:
        right = (slab // bit) % 2 == 1

        def sides(own):
            seen = partner(own, bit)
            return jnp.where(right, seen, own), jnp.where(right, own, seen)

        (ax, ay), (cx, cy), (dx, dy) = sides(a_map), sides(c_map), sides(d_map)
        (wx, wy), (fx, fy) = sides(shift), sides(first)
        (px, py), (qx, qy) = sides(leave), sides(back)
        middle = px + compute(wx, fy)
        entry = qy + compute(dy, middle)
        carried = compute(dy, ax)
        pi = pi + jnp.where(right, compute(alpha, middle), 0.0)
        sigma = sigma + jnp.where(right, compute(delta, middle), compute(gamma, entry))
        delta = jnp.where(right, compute(delta, ax), delta + compute(gamma, carried))
        alpha = jnp.where(right, compute(alpha, ax), alpha)
        gamma = jnp.where(right, gamma, compute(gamma, cy))
        leave, back = py + compute(ay, middle), qx + compute(cx, entry)
        a_map, c_map, d_map = compute(ay, ax), compute(cx, cy), dx + compute(cx, carried)
        shift, first = wy, fx
        bit *= 2
        if 2 * bit == slabs:
            left = slab < slabs // 2
            send = jnp.concatenate([jnp.where(left, leave, back), first], axis=0).astype(BF16)
            send_map = lax.dynamic_slice_in_dim(
                jnp.where(left, shift, d_map).astype(BF16),
                row * half,
                half,
                0,
            )
            first = first.astype(BF16)
            leaving = jnp.concatenate([leave, leave], axis=0)
            response = jnp.concatenate(
                [lax.dynamic_slice_in_dim(x, row * half, half, 0) for x in (alpha, delta)], axis=0
            )
    map_seen = partner(send_map, slabs // 2)
    seen = partner(send, slabs // 2)
    response_other = across(response)
    map_other = across(map_seen)
    hand, base = call(
        ready_kernel,
        [V] * 6,
        [((4, 2 * surface, 2 * surface), BF16), (thin, F32)],
        [((2,) + square, F32)],
        couple_near,
        sigma,
        response,
        response_other,
        gamma,
        shift,
    )
    ends, ahead_map = call(
        merge_kernel,
        [V] * 7,
        [((2,) + thin, F32), ((2, 2 * surface, 2 * surface), BF16)],
        [(square, BF16)],
        hand,
        base,
        pi,
        leaving,
        first,
        map_seen,
        map_other,
    )
    (closed,) = call(
        close_kernel, [V] * 4, [((columns, 2 * surface), BF16)], [], hand, ends, ahead_map, seen
    )
    (result,) = call(
        final_kernel,
        [V] * 5,
        [((2, shard_rows, columns), F32)],
        [((2, columns, 2 * surface), BF16)],
        count,
        green_blocks,
        direct,
        closed,
        across(closed),
        keep=True,
    )
    return result


def solution(mesh):
    placed = (
        P(None, ("energy", "slab", "row"), None),
        P(None, "slab", None),
        P(None, ("energy", "slab", "row"), None),
        P("slab"),
    )
    return jax.shard_map(
        body,
        mesh=mesh,
        in_specs=placed,
        out_specs=P(None, ("energy", "slab", "row"), None),
        check_vma=False,
    )
```
